256 devices in a mesh: cuts: 64 (over x, y, z_lo), frame: 4 (over z_hi, core).
Axes of the slice: x: 4, y: 4, z: 8 (z_hi: 2, z_lo: 4; z = z_hi * 4 + z_lo), core: 2. Of those that a mesh axis runs over, the one named last changes fastest.
Arguments:
- basis: bfloat16 [2, 32, 128, 4, 256], P(None, None, 'cuts', 'frame'), may hold values from -6 to 6
- coil_maps: bfloat16 [2, 12, 128, 4, 256], P(None, None, 'cuts', 'frame'), may hold values from -3 to 3
- factors: bfloat16 [2, 32, 64], P(None, None, 'frame'), may hold values from -0.75 to 0.75
- lines: int32 [64, 128], P(None, 'cuts'), may hold values from 0 to 511
- kdata: bfloat16 [2, 64, 128, 12, 4], P(None, None, 'cuts', None, 'frame'), may hold values from -6 to 6
Outputs:
- basis_grad: float32 [2, 32, 128, 4, 256], P(None, None, 'cuts', 'frame')
- factor_grad: float32 [2, 32, 64], P(None, None, 'frame')
The draws below stay inside these ranges and needn't reach their ends.
Inputs may be any that keep to these rules, and one draw needn't show every extreme that they name: lines[t, j] = (ky - (j // 2) * 4) * 128 + kz for a position (ky, kz) sampled in frame t whose ky lies in the rows (j // 2) * 4 to (j // 2 + 1) * 4 - 1; positions may repeat over frames.
All inputs are finite; a program needn't handle non-finite values.
Results may differ from the reference program's by a relative error of at most 0.011.
Values may be sent and summed in bfloat16 or wider, within the bound.
A program may use at most 64 MiB of HBM per device.

```python
import math
import jax
import jax.numpy as jnp
from jax import lax

RANK = 32
COILS = 12
NY = 256
NZ = 128
LPD = 2
NXW = 4
FRAMES = 64
LINES = 128
RY = 4


def plant(entries, own_key, smallest, top_value):
    extent = entries.shape
    place = [jax.random.randint(jax.random.fold_in(own_key, axis), (), 0, extent[axis]) for axis in range(len(extent))]
    entries = entries.at[tuple(place)].set(smallest)
    longest = extent.index(max(extent))
    place[longest] = (place[longest] + 1) % extent[longest]
    return entries.at[tuple(place)].set(top_value)


def level_of(own_key, extent, shards, low, largest):
    gain = 1.0
    for position, shards_of in shards:
        draws = jax.random.uniform(jax.random.fold_in(jax.random.fold_in(own_key, 6), position), (shards_of,), jnp.float32, low / len(shards), largest / len(shards))
        gain = gain * jnp.repeat(jnp.exp(draws), extent[position] // shards_of).reshape((-1,) + (1,) * (len(extent) - 1 - position))
    return gain


def bell_draw(key, shape, deviation, most, shards=(), kind=jnp.bfloat16):
    gain = level_of(key, shape, shards, -0.22, 0.18) if shards else 1.0
    result = jax.random.normal(key, shape, jnp.float32) * deviation * gain
    return jnp.minimum(jnp.maximum(result, -most), most).astype(kind)


def setup_inputs(seed: int = 0) -> dict:
    splits = jax.random.split(jax.random.key(seed), 6)
    basis = bell_draw(splits[0], (2, RANK, NZ, NXW, NY), 1.0, 6.0, ((2, 64), (3, 4)))
    coil_maps = bell_draw(splits[1], (2, COILS, NZ, NXW, NY), 0.5, 3.0, ((2, 64), (3, 4)))
    factors = bell_draw(splits[2], (2, RANK, FRAMES), (2 * RANK) ** -0.5, 0.75, ((2, 4),))
    lines = plant(jax.random.randint(splits[3], (FRAMES, LINES), 0, RY * NZ), jax.random.fold_in(splits[3], 1), 0, (RY * NZ) - 1).astype(jnp.int32)
    kdata = bell_draw(splits[4], (2, FRAMES, LINES, COILS, NXW), 1.0, 6.0, ((2, 64), (4, 4)))
    return {"basis": basis, "coil_maps": coil_maps, "factors": factors, "lines": lines, "kdata": kdata}


HIGH = lax.Precision.HIGHEST

def twiddle(product, size):
    angle = product.astype(jnp.float32) * (2.0 * math.pi / size)
    factor = 1.0 / math.sqrt(size)
    return ((jnp.cos(angle) * factor).astype(jnp.bfloat16), (jnp.sin(angle) * factor).astype(jnp.bfloat16))

def dft_table(size, inverse):
    index = jnp.arange(size, dtype=jnp.int32)
    product = index[:, None] * index[None, :] % size
    cosine, sine = twiddle(product, size)
    imag = sine if inverse else -sine
    return jnp.stack([jnp.stack([cosine, imag]), jnp.stack([-imag, cosine])])

def rounded(value):
    return lax.optimization_barrier(value.astype(jnp.bfloat16)).astype(jnp.float32)

def reference(basis, coil_maps, factors, lines, kdata):
    fwd_y = dft_table(NY, False).astype(jnp.float32)
    inv_y = dft_table(NY, True).astype(jnp.float32)
    fwd_z = dft_table(NZ, False).astype(jnp.float32)
    inv_z = dft_table(NZ, True).astype(jnp.float32)
    column = jnp.arange(LINES, dtype=jnp.int32) // LPD
    ky_pos = column[None, :] * RY + lines // NZ
    kz_pos = lines % NZ
    v_re = factors[0].astype(jnp.float32)
    v_im = factors[1].astype(jnp.float32)
    b_re = basis[0].astype(jnp.float32)
    b_im = basis[1].astype(jnp.float32)
    scale = 1.0 / math.sqrt(COILS * LINES * NXW)

    def per_coil(carry, inputs):
        grad_acc, factor_acc = carry
        maps, data = inputs
        m_re = maps[0].astype(jnp.float32)[None]
        m_im = maps[1].astype(jnp.float32)[None]
        image = rounded(jnp.stack([m_re * b_re - m_im * b_im, m_re * b_im + m_im * b_re]))
        hybrid = rounded(jnp.einsum('plzxy,pqwy->qlzxw', image, fwd_y, precision=HIGH))
        kspace = jnp.einsum('plzxy,pqkz->qlkxy', hybrid, fwd_z, precision=HIGH)
        turned = kspace.transpose(2, 4, 0, 1, 3)
        picked = turned[kz_pos, ky_pos]
        p_re = picked[:, :, 0]
        p_im = picked[:, :, 1]
        pred_re = jnp.einsum('tjlx,lt->tjx', p_re, v_re, precision=HIGH) - jnp.einsum('tjlx,lt->tjx', p_im, v_im, precision=HIGH)
        pred_im = jnp.einsum('tjlx,lt->tjx', p_re, v_im, precision=HIGH) + jnp.einsum('tjlx,lt->tjx', p_im, v_re, precision=HIGH)
        resid = rounded(jnp.stack([pred_re, pred_im]) - data.astype(jnp.float32))
        r_re = resid[0]
        r_im = resid[1]
        gv_re = jnp.einsum('tjlx,tjx->lt', p_re, r_re, precision=HIGH) + jnp.einsum('tjlx,tjx->lt', p_im, r_im, precision=HIGH)
        gv_im = jnp.einsum('tjlx,tjx->lt', p_re, r_im, precision=HIGH) - jnp.einsum('tjlx,tjx->lt', p_im, r_re, precision=HIGH)
        vt_re = v_re.T[:, None, :, None]
        vt_im = v_im.T[:, None, :, None]
        val_re = r_re[:, :, None, :] * vt_re + r_im[:, :, None, :] * vt_im
        val_im = r_im[:, :, None, :] * vt_re - r_re[:, :, None, :] * vt_im
        values = jnp.stack([val_re, val_im], axis=2)
        kgrad = jnp.zeros((NZ, NY, 2, RANK, NXW), jnp.float32).at[kz_pos, ky_pos].add(values)
        zgrad = rounded(jnp.einsum('kwplx,pqzk->qlzxw', kgrad, inv_z, precision=HIGH))
        imgrad = jnp.einsum('plzxw,pqyw->qlzxy', zgrad, inv_y, precision=HIGH)
        g_re = imgrad[0]
        g_im = imgrad[1]
        update = jnp.stack([m_re * g_re + m_im * g_im, m_re * g_im - m_im * g_re])
        return ((grad_acc + update, factor_acc + jnp.stack([gv_re, gv_im])), None)
    start = (jnp.zeros((2, RANK, NZ, NXW, NY), jnp.float32), jnp.zeros((2, RANK, FRAMES), jnp.float32))
    inputs = (coil_maps.transpose(1, 0, 2, 3, 4), kdata.transpose(3, 0, 1, 2, 4))
    (grad_acc, factor_acc), unused = lax.scan(per_coil, start, inputs)
    return (grad_acc, factor_acc * scale)
```

```python
import math

import jax
import jax.numpy as jnp
import numpy as np
from jax import lax
from jax.sharding import PartitionSpec as P

BF = jnp.bfloat16
F32 = jnp.float32


def dft_np(size):
    index = np.arange(size)
    angle = (index[:, None] * index[None, :] % size) * (2.0 * math.pi / size)
    return np.cos(angle) / math.sqrt(size), -np.sin(angle) / math.sqrt(size)


def dot(spec, a, b):
    return jnp.einsum(spec, a, b, preferred_element_type=F32)


def body(basis, coil_maps, factors, lines, kdata):
    n_cuts = lax.axis_size("cuts")
    cuts = lax.axis_index("cuts")
    rank, slab, width = basis.shape[1], basis.shape[2], basis.shape[4]
    coils = coil_maps.shape[1]
    depth = slab * n_cuts
    rows = width // n_cuts
    lpd = lines.shape[1]
    scale = 1.0 / math.sqrt(coils * lpd * n_cuts * basis.shape[3] * lax.axis_size("frame"))
    cy, sy = dft_np(width)
    perm = (np.arange(rows)[:, None] + rows * np.arange(n_cuts)[None, :]).reshape(-1)
    c, s = cy[:, perm], sy[:, perm]
    table = jnp.asarray(np.block([[c, s], [-s, c]]), BF)

    v = lax.all_gather(factors, "frame", axis=2, tiled=True)
    frames = v.shape[2]
    every = lax.all_gather(lines, "cuts", axis=0)
    kz = every % depth
    row = every // depth
    b = basis[:, :, :, 0].astype(F32)
    m = coil_maps[:, :, :, 0].astype(F32)
    image = jnp.stack(
        [
            m[0][:, :, None] * b[0].transpose(1, 0, 2)[None] - m[1][:, :, None] * b[1].transpose(1, 0, 2)[None],
            m[0][:, :, None] * b[1].transpose(1, 0, 2)[None] + m[1][:, :, None] * b[0].transpose(1, 0, 2)[None],
        ],
        axis=3,
    ).astype(BF)
    image = image.reshape(coils * slab * rank, 2 * width)
    hybrid = jnp.dot(image, table, preferred_element_type=F32).astype(BF)
    hybrid = hybrid.reshape(coils, slab, rank, 2, width)
    vr, vi = v[0], v[1]
    mixer = jnp.stack([jnp.stack([vr, -vi]), jnp.stack([vi, vr])])
    mixed = dot("czlpw,qplt->czqtw", hybrid, mixer).reshape(coils, slab, 2, frames, rows, n_cuts)
    zpos = cuts * slab + jnp.arange(slab)
    angle = (kz[None] * zpos[:, None, None, None] % depth).astype(F32) * (2.0 * math.pi / depth)
    pr = (jnp.cos(angle) / math.sqrt(depth)).astype(BF).astype(F32)
    pi = (-jnp.sin(angle) / math.sqrt(depth)).astype(BF).astype(F32)
    pr = pr.transpose(0, 3, 2, 1)
    pi = pi.transpose(0, 3, 2, 1)
    row = row.transpose(2, 1, 0)
    parts = []
    for sample in range(lpd):
        r = row[sample]
        sel = sum(
            jnp.where(r == k, mixed[:, :, :, :, k], 0.0) for k in range(rows)
        )
        re = jnp.sum(sel[:, :, 0] * pr[None, :, sample] - sel[:, :, 1] * pi[None, :, sample], 1)
        im = jnp.sum(sel[:, :, 0] * pi[None, :, sample] + sel[:, :, 1] * pr[None, :, sample], 1)
        parts.append(jnp.stack([re, im]))
    part = jnp.stack(parts)
    part = part.transpose(4, 2, 1, 0, 3).reshape(n_cuts, -1).astype(BF)
    pred = lax.psum_scatter(part, "cuts", scatter_dimension=0, tiled=True)
    kd = kdata[..., 0].transpose(3, 0, 2, 1).reshape(1, -1)
    resid = (pred.astype(F32) - kd.astype(F32)).astype(BF)
    whole = lax.all_gather(resid, "cuts", axis=0, tiled=True)
    whole = whole.reshape(n_cuts, coils, 2, lpd, frames).transpose(3, 2, 1, 4, 0).astype(F32)
    spread = 0.0
    for sample in range(lpd):
        x, y = whole[sample, 0][:, None], whole[sample, 1][:, None]
        re = x * pr[None, :, sample] + y * pi[None, :, sample]
        im = y * pr[None, :, sample] - x * pi[None, :, sample]
        e = jnp.stack([re, im], 2)
        r = row[sample]
        spread = spread + jnp.stack([jnp.where(r == k, e, 0.0) for k in range(rows)], 4)
    spread = spread.astype(BF).reshape(coils, slab, 2, frames, width)
    outer = dot("czlpw,czqtw->plqt", hybrid, spread)
    gv = jnp.stack([outer[0, :, 0] + outer[1, :, 1], outer[0, :, 1] - outer[1, :, 0]])
    unmix = jnp.stack([jnp.stack([vr, vi]), jnp.stack([-vi, vr])])
    zgrad = dot("czptw,qplt->czlqw", spread, unmix).astype(BF)
    zgrad = zgrad.reshape(coils * slab * rank, 2 * width)
    back = lax.dot_general(zgrad, table, (((1,), (1,)), ((), ())), preferred_element_type=F32)
    back = back.reshape(coils, slab, rank, 2, width)
    gr = jnp.sum(m[0][:, :, None] * back[:, :, :, 0] + m[1][:, :, None] * back[:, :, :, 1], 0)
    gi = jnp.sum(m[0][:, :, None] * back[:, :, :, 1] - m[1][:, :, None] * back[:, :, :, 0], 0)
    grad = jnp.stack([gr, gi]).transpose(0, 2, 1, 3)[:, :, :, None]
    shared = lax.psum_scatter(gv * scale, "frame", scatter_dimension=2, tiled=True)
    return grad, lax.psum(shared, "cuts")


def solution(mesh):
    placed = (
        P(None, None, "cuts", "frame", None),
        P(None, None, "cuts", "frame", None),
        P(None, None, "frame"),
        P(None, "cuts"),
        P(None, None, "cuts", None, "frame"),
    )
    return jax.shard_map(
        body,
        mesh=mesh,
        in_specs=placed,
        out_specs=(P(None, None, "cuts", "frame", None), P(None, None, "frame")),
        check_vma=False,
    )
```

```python
import functools
import math

import jax
import jax.numpy as jnp
import numpy as np
from jax import lax
from jax.experimental import pallas as pl
from jax.experimental.pallas import tpu as pltpu
from jax.sharding import PartitionSpec as P

BF = jnp.bfloat16
F32 = jnp.float32
I32 = jnp.int32
GROUP = 4
ROWS = 4


def real_table(size, blocks):
    index = np.arange(size)
    angle = (index[:, None] * index[None, :] % size) * (2.0 * math.pi / size)
    cosine, sine = np.cos(angle) / math.sqrt(size), np.sin(angle) / math.sqrt(size)
    order = (np.arange(ROWS)[:, None] + ROWS * np.arange(blocks)[None, :]).reshape(-1)
    c, s = cosine[order], sine[order]
    return np.block([[c, s], [-s, c]])


def nn(a, b):
    return jnp.dot(a, b, preferred_element_type=F32)


def nt(a, b):
    return lax.dot_general(a, b, (((1,), (1,)), ((), ())), preferred_element_type=F32)


def iota(shape, axis):
    return lax.broadcasted_iota(I32, shape, axis)


def kernel(
    dims,
    scale,
    b_ref,
    m_ref,
    v_ref,
    l_ref,
    d_ref,
    t_ref,
    grad_ref,
    fg_ref,
    img,
    ht,
    hn,
    pb,
    vbt,
    vc,
    ph,
    rowid,
    perm,
    permt,
    sx,
    xr,
    sy,
    yr,
    sz,
    zr,
    ra,
    lg,
    vg,
    kg,
    kd,
    zg,
    gv,
    gs,
    gr,
    send,
    rx,
    ry,
    rz,
    ray,
    rax,
    rl,
    rv,
    rk,
    rg,
):
    na, nb, nc, nf, chunks = dims
    slab, parts, rank, width = b_ref.shape
    frames = 64
    blocks = na * nb * nc
    depth = slab * blocks
    me = lax.axis_index("cuts")
    fr = lax.axis_index("frame")
    ia, ib, ic = me // (nb * nc), (me // nc) % nb, me % nc
    lane = 2 * frames
    sl = slab * rank

    def peer_a(j):
        return {"cuts": lax.rem(ia + j, na) * (nb * nc) + ib * nc + ic}

    def peer_b(j):
        return {"cuts": ia * (nb * nc) + lax.rem(ib + j, nb) * nc + ic}

    def peer_c(j):
        return {"cuts": ia * (nb * nc) + ib * nc + lax.rem(ic + j, nc)}

    def peer_f(j):
        return {"frame": lax.rem(fr + j, nf)}

    def remote(src, dst, s, r, who):
        return pltpu.make_async_remote_copy(
            src_ref=src,
            dst_ref=dst,
            send_sem=s,
            recv_sem=r,
            device_id=who,
            device_id_type=pl.DeviceIdType.MESH,
        )

    everyone = (
        [peer_a(j) for j in range(1, na)]
        + [peer_b(j) for j in range(1, nb)]
        + [peer_c(j) for j in range(1, nc)]
        + [peer_f(j) for j in range(1, nf)]
    )
    barrier = pltpu.get_barrier_semaphore()
    for who in everyone:
        pl.semaphore_signal(barrier, inc=1, device_id=who, device_id_type=pl.DeviceIdType.MESH)

    lg[pl.ds(me, 1)] = l_ref[...][None]
    vg[pl.ds(fr, 1)] = v_ref[...][None]
    kg[pl.ds(ic, 1)] = d_ref[...][None]

    n_rows = GROUP * blocks
    out_row = iota((n_rows, n_rows), 0)
    in_row = iota((n_rows, n_rows), 1)

    def spot(r):
        return (r // nc) % GROUP * blocks + r // (nc * GROUP) * nc + r % nc

    perm[...] = (spot(out_row) == in_row).astype(F32).astype(BF)
    permt[...] = (spot(in_row) == out_row).astype(F32).astype(BF)

    def forward(k, carry):
        for c4 in range(GROUP):
            for z in range(slab):
                base = ((k * GROUP + c4) * slab + z) * 2
                mr, mi = m_ref[base], m_ref[base + 1]
                br, bi = b_ref[z, 0].astype(F32), b_ref[z, 1].astype(F32)
                at = (c4 * slab + z) * rank
                img[k, at : at + rank, 0:width] = (mr * br - mi * bi).astype(BF)
                img[k, at : at + rank, width : 2 * width] = (mr * bi + mi * br).astype(BF)
        ht[k] = nt(t_ref[...], img[k]).astype(BF)
        return carry

    lax.fori_loop(0, chunks, forward, 0)

    pl.semaphore_wait(barrier, len(everyone))

    vcopies = [
        remote(vg.at[fr], vg.at[fr], send.at[0, j], rv.at[j], peer_f(j)) for j in range(1, nf)
    ]
    lc = [
        remote(lg.at[pl.ds(me, 1)], lg.at[pl.ds(me, 1)], send.at[1, j], rl.at[0, j], peer_c(j))
        for j in range(1, nc)
    ]
    kcopies = [
        remote(kg.at[ic], kg.at[ic], send.at[2, j], rk.at[j], peer_c(j)) for j in range(1, nc)
    ]
    for copy in lc + vcopies + kcopies:
        copy.start()
    for copy in lc:
        copy.wait()
    low = (ia * nb + ib) * nc
    lb = [
        remote(lg.at[pl.ds(low, nc)], lg.at[pl.ds(low, nc)], send.at[3, j], rl.at[1, j], peer_b(j))
        for j in range(1, nb)
    ]
    for copy in lb:
        copy.start()
    for copy in vcopies:
        copy.wait()

    vt = [vg[:, p].reshape(frames, rank) for p in range(2)]
    rep = (iota((rank, 4 * rank), 0) == iota((rank, 4 * rank), 1) % rank).astype(F32).astype(BF)
    wide = [nn(vt[p], rep) for p in range(2)]
    block_of = iota((frames, 4 * rank), 1) // rank
    for blk in range(4):
        r_ = jnp.where(block_of == blk, wide[0], 0.0).astype(BF)
        i_ = jnp.where(block_of == blk, wide[1], 0.0).astype(BF)
        at = blk * frames
        vbt[at : at + frames, 0 : 4 * rank] = r_
        vbt[at : at + frames, 4 * rank : 8 * rank] = -i_
        at = (4 + blk) * frames
        vbt[at : at + frames, 0 : 4 * rank] = i_
        vbt[at : at + frames, 4 * rank : 8 * rank] = r_
    rep2 = (iota((sl, rank), 0) % rank == iota((sl, rank), 1)).astype(F32).astype(BF)
    same = iota((sl, lane), 0) // rank == iota((sl, lane), 1) // frames
    tall = [nt(rep2, jnp.concatenate([vt[p], vt[p]], 0)) for p in range(2)]
    r_ = jnp.where(same, tall[0], 0.0).astype(BF)
    i_ = jnp.where(same, tall[1], 0.0).astype(BF)
    vc[0:sl, 0:lane] = r_
    vc[0:sl, lane : 2 * lane] = i_
    vc[sl : 2 * sl, 0:lane] = -i_
    vc[sl : 2 * sl, lane : 2 * lane] = r_

    for copy in lb:
        copy.wait()
    low = ia * nb * nc
    la = [
        remote(
            lg.at[pl.ds(low, nb * nc)],
            lg.at[pl.ds(low, nb * nc)],
            send.at[4, j],
            rl.at[2, j],
            peer_a(j),
        )
        for j in range(1, na)
    ]
    for copy in la:
        copy.start()

    def again(k, carry):
        full = nt(img[k], t_ref[...]).astype(BF)
        for c4 in range(GROUP):
            hn[k, c4, 0:sl, :] = full[c4 * sl : (c4 + 1) * sl, 0:width]
            hn[k, c4, sl : 2 * sl, :] = full[c4 * sl : (c4 + 1) * sl, width : 2 * width]
        return carry

    lax.fori_loop(0, chunks, again, 0)

    for copy in kcopies:
        copy.wait()
    kall = kg[...].reshape(nc * 16, 2 * lane)
    krow = iota((chunks * GROUP * nc, nc * 16), 0)
    kcol = iota((chunks * GROUP * nc, nc * 16), 1)
    pick = (krow % nc * 16 + krow // nc == kcol).astype(F32).astype(BF)
    kd[...] = nn(pick, kall).reshape(chunks, GROUP * nc, 2 * lane)

    for copy in la:
        copy.wait()

    lo = iota((blocks, lane), 1) < frames
    every = lg[...].reshape(blocks, lane)
    turned = pltpu.roll(every, frames, 1)
    zpos = me * slab + iota((blocks, lane), 1) // frames
    norm = 1.0 / math.sqrt(depth)
    for s in range(2):
        mine = jnp.where(lo, every, turned) if s == 0 else jnp.where(lo, turned, every)
        kz = lax.rem(mine, depth)
        rowid[s] = lax.div(mine, depth)
        angle = lax.rem(kz * zpos, depth).astype(F32) * (2.0 * math.pi / depth)
        ph[s, 0] = (jnp.cos(angle) * norm).astype(BF).astype(F32)
        ph[s, 1] = (jnp.sin(angle) * -norm).astype(BF).astype(F32)

    def parts_of(k, carry):
        for pair in range(GROUP // 2):
            at = pair * 2 * sl
            lhs = jnp.concatenate(
                [ht[k, 0:width, at : at + 2 * sl], ht[k, width : 2 * width, at : at + 2 * sl]], 1
            )
            mixed = nt(lhs, vbt[...])
            for c2 in range(2):
                re0, im0 = c2 * lane, (2 + c2) * lane
                got = []
                for s in range(2):
                    rs = rowid[s]
                    mr = mixed[0:blocks, re0 : re0 + lane]
                    mi = mixed[0:blocks, im0 : im0 + lane]
                    for r in range(1, ROWS):
                        here = rs == r
                        mr = jnp.where(here, mixed[r * blocks : (r + 1) * blocks, re0 : re0 + lane], mr)
                        mi = jnp.where(here, mixed[r * blocks : (r + 1) * blocks, im0 : im0 + lane], mi)
                    pr, pi = ph[s, 0], ph[s, 1]
                    got.append((pr * mr - pi * mi, pr * mi + pi * mr))
                row = (pair * 2 + c2) * blocks
                for q in range(2):
                    keep = jnp.where(lo, got[0][q], got[1][q])
                    fold = jnp.where(lo, got[1][q], got[0][q])
                    total = keep + pltpu.roll(fold, frames, 1)
                    pb[row : row + blocks, q * lane : (q + 1) * lane] = total.astype(BF)
        part = nn(perm[...], pb[...]).astype(BF)
        sx[k] = part.reshape(na, nb, GROUP * nc, 2 * lane)
        for j in range(1, na):
            to_a(k, j).start()
        return carry

    def to_a(k, j):
        return remote(
            sx.at[k, lax.rem(ia + j, na)], xr.at[k, j], send.at[5 + k, j], rx.at[k, j], peer_a(j)
        )

    def to_b(k, j):
        return remote(
            sy.at[k, lax.rem(ib + j, nb)], yr.at[k, j], send.at[8 + k, j], ry.at[k, j], peer_b(j)
        )

    def to_c(k, j):
        return remote(sz.at[k], zr.at[k, j], send.at[11 + k, j], rz.at[k, j], peer_c(j))

    def back_b(k, j):
        return remote(
            ra.at[k, ia, ib], ra.at[k, ia, ib], send.at[14 + k, j], ray.at[k, j], peer_b(j)
        )

    def back_a(k, j):
        return remote(ra.at[k, ia], ra.at[k, ia], send.at[17 + k, j], rax.at[k, j], peer_a(j))

    lax.fori_loop(0, chunks, parts_of, 0)

    for k in range(chunks):
        total = sx[k, ia].astype(F32)
        for j in range(1, na):
            to_a(k, j).wait()
            total = total + xr[k, j].astype(F32)
        sy[k] = total.astype(BF)
        for j in range(1, nb):
            to_b(k, j).start()
    for k in range(chunks):
        total = sy[k, ib].astype(F32)
        for j in range(1, nb):
            to_b(k, j).wait()
            total = total + yr[k, j].astype(F32)
        sz[k] = total.astype(BF)
        for j in range(1, nc):
            to_c(k, j).start()
    for k in range(chunks):
        total = sz[k].astype(F32)
        for j in range(1, nc):
            to_c(k, j).wait()
            total = total + zr[k, j].astype(F32)
        ra[k, ia, ib] = (total - kd[k]).astype(BF)
        for j in range(1, nb):
            back_b(k, j).start()
    for k in range(chunks):
        for j in range(1, nb):
            back_b(k, j).wait()
        for j in range(1, na):
            back_a(k, j).start()

    grad_ref[...] = jnp.zeros_like(grad_ref)
    gv[...] = jnp.zeros_like(gv)

    def backward(k, carry):
        for j in range(1, na):
            back_a(k, j).wait()
        resid = nn(permt[...], ra[k].reshape(n_rows, 2 * lane))
        for c4 in range(GROUP):
            here = [resid[c4 * blocks : (c4 + 1) * blocks, q * lane : (q + 1) * lane] for q in range(2)]
            flip = [pltpu.roll(x, frames, 1) for x in here]
            terms = []
            for s in range(2):
                xr_, xi_ = [
                    jnp.where(lo, a, b) if s == 0 else jnp.where(lo, b, a) for a, b in zip(here, flip)
                ]
                pr, pi = ph[s, 0], ph[s, 1]
                terms.append((xr_ * pr + xi_ * pi, xi_ * pr - xr_ * pi))
            spread = []
            for r in range(ROWS):
                m0, m1 = rowid[0] == r, rowid[1] == r
                spread.append(
                    jnp.concatenate(
                        [
                            (
                                jnp.where(m0, terms[0][q], 0.0) + jnp.where(m1, terms[1][q], 0.0)
                            ).astype(BF)
                            for q in range(2)
                        ],
                        1,
                    )
                )
            e = jnp.concatenate(spread, 0)
            zc = nt(vc[...], e).astype(BF)
            zg[c4 * sl : (c4 + 1) * sl, 0:width] = zc[0:sl]
            zg[c4 * sl : (c4 + 1) * sl, width : 2 * width] = zc[sl : 2 * sl]
            gv[...] += nn(hn[k, c4], e)
        back = nn(zg[...], t_ref[...])
        for z in range(slab):
            re, im = grad_ref[0, z], grad_ref[1, z]
            for c4 in range(GROUP):
                base = ((k * GROUP + c4) * slab + z) * 2
                mr, mi = m_ref[base], m_ref[base + 1]
                at = (c4 * slab + z) * rank
                br = back[at : at + rank, 0:width]
                bi = back[at : at + rank, width : 2 * width]
                re = re + mr * br + mi * bi
                im = im + mr * bi - mi * br
            grad_ref[0, z], grad_ref[1, z] = re, im
        return carry

    lax.fori_loop(0, chunks, backward, 0)

    g = gv[...]
    own = {}
    for p in range(2):
        for q in range(2):
            first = g[p * sl : p * sl + rank, q * lane : (q + 1) * lane]
            second = g[p * sl + rank : (p + 1) * sl, q * lane : (q + 1) * lane]
            own[p, q] = first + pltpu.roll(second, frames, 1)
    gre = (own[0, 0] + own[1, 1]) * scale
    gim = (own[0, 1] - own[1, 0]) * scale
    turned = jnp.transpose(jnp.concatenate([gre, gim, gre, gim], 0))
    span = frames // nf
    gs[0:nf] = turned[0:frames].reshape(nf, span, 4 * rank)

    copies = [
        remote(gs.at[lax.rem(fr + j, nf)], gr.at[0, j], send.at[20, j], rg.at[0, j], peer_f(j))
        for j in range(1, nf)
    ]
    for copy in copies:
        copy.start()
    total = gs[fr]
    for j, copy in enumerate(copies):
        copy.wait()
        total = total + gr[0, j + 1]
    for level, (count, peer) in enumerate(((nc, peer_c), (nb, peer_b), (na, peer_a))):
        gs[nf + level] = total
        copies = [
            remote(
                gs.at[nf + level],
                gr.at[1 + level, j],
                send.at[21 + level, j],
                rg.at[1 + level, j],
                peer(j),
            )
            for j in range(1, count)
        ]
        for copy in copies:
            copy.start()
        for j, copy in enumerate(copies):
            copy.wait()
            total = total + gr[1 + level, j + 1]
    fg_ref[...] = total


SHAPES = {64: (4, 4, 4), 8: (2, 2, 2)}


def body(basis, coil_maps, factors, lines, kdata):
    n_cuts = lax.axis_size("cuts")
    nf = lax.axis_size("frame")
    na, nb, nc = SHAPES[n_cuts]
    rank, slab, width = basis.shape[1], basis.shape[2], basis.shape[4]
    coils = coil_maps.shape[1]
    chunks = coils // GROUP
    span = factors.shape[2]
    lpd = lines.shape[1]
    frames = span * nf
    lane = 2 * frames
    sl = slab * rank
    blocks = n_cuts
    n_rows = GROUP * blocks
    scale = 1.0 / math.sqrt(coils * lpd * n_cuts * basis.shape[3] * nf)
    table = jnp.asarray(real_table(width, n_cuts), BF)
    b = basis[:, :, :, 0].transpose(2, 0, 1, 3)
    m = coil_maps[:, :, :, 0].transpose(1, 2, 0, 3).reshape(coils * slab * 2, 1, width).astype(F32)
    v = factors.transpose(0, 2, 1)
    l = lines.T.reshape(1, lane)
    d = jnp.pad(kdata[..., 0].transpose(3, 0, 2, 1).reshape(coils, 2 * lane), ((0, 16 - coils), (0, 0)))
    dma = pltpu.SemaphoreType.DMA
    vm = pltpu.VMEM
    scratch = [
        vm((chunks, GROUP * sl, 2 * width), BF),
        vm((chunks, 2 * width, GROUP * sl), BF),
        vm((chunks, GROUP, 2 * sl, width), BF),
        vm((n_rows, 2 * lane), BF),
        vm((8 * frames, 8 * rank), BF),
        vm((2 * sl, 2 * lane), BF),
        vm((2, 2, blocks, lane), F32),
        vm((2, blocks, lane), I32),
        vm((n_rows, n_rows), BF),
        vm((n_rows, n_rows), BF),
        vm((chunks, na, nb, GROUP * nc, 2 * lane), BF),
        vm((chunks, na, nb, GROUP * nc, 2 * lane), BF),
        vm((chunks, nb, GROUP * nc, 2 * lane), BF),
        vm((chunks, nb, GROUP * nc, 2 * lane), BF),
        vm((chunks, GROUP * nc, 2 * lane), BF),
        vm((chunks, nc, GROUP * nc, 2 * lane), BF),
        vm((chunks, na, nb, GROUP * nc, 2 * lane), BF),
        vm((blocks, 1, lane), I32),
        vm((nf, 2, span, rank), BF),
        vm((nc, 16, 2 * lane), BF),
        vm((chunks, GROUP * nc, 2 * lane), F32),
        vm((GROUP * sl, 2 * width), BF),
        vm((2 * sl, 2 * lane), F32),
        vm((nf + 3, span, 4 * rank), F32),
        vm((4, 4, span, 4 * rank), F32),
        dma((24, 4)),
        dma((3, 4)),
        dma((3, 4)),
        dma((3, 4)),
        dma((3, 4)),
        dma((3, 4)),
        dma((3, 4)),
        dma((4,)),
        dma((4,)),
        dma((4, 4)),
    ]
    grad, fg = pl.pallas_call(
        functools.partial(kernel, (na, nb, nc, nf, chunks), scale),
        out_shape=(
            jax.ShapeDtypeStruct((2, slab, rank, width), F32),
            jax.ShapeDtypeStruct((span, 4 * rank), F32),
        ),
        in_specs=[pl.BlockSpec(memory_space=pltpu.VMEM)] * 6,
        out_specs=[pl.BlockSpec(memory_space=pltpu.VMEM)] * 2,
        scratch_shapes=scratch,
        compiler_params=pltpu.CompilerParams(
            collective_id=0, has_side_effects=True, vmem_limit_bytes=56 * 1024 * 1024
        ),
    )(b, m, v, l, d, table)
    grad = grad.transpose(0, 2, 1, 3)[:, :, :, None]
    fg = fg[:, : 2 * rank].reshape(span, 2, rank).transpose(1, 2, 0)
    return grad, fg


def solution(mesh):
    placed = (
        P(None, None, "cuts", "frame", None),
        P(None, None, "cuts", "frame", None),
        P(None, None, "frame"),
        P(None, "cuts"),
        P(None, None, "cuts", None, "frame"),
    )
    return jax.shard_map(
        body,
        mesh=mesh,
        in_specs=placed,
        out_specs=(P(None, None, "cuts", "frame", None), P(None, None, "frame")),
        check_vma=False,
    )
```

```python
import functools
import math

import jax
import jax.numpy as jnp
import numpy as np
from jax import lax
from jax.experimental import pallas as pl
from jax.experimental.pallas import tpu as pltpu
from jax.sharding import PartitionSpec as P

BF = jnp.bfloat16
F32 = jnp.float32
I32 = jnp.int32
GROUP = 4
ROWS = 4


def real_table(size, shape):
    index = np.arange(size)
    angle = (index[:, None] * index[None, :] % size) * (2.0 * math.pi / size)
    cosine, sine = np.cos(angle) / math.sqrt(size), np.sin(angle) / math.sqrt(size)
    block = np.arange(np.prod(shape)).reshape(shape).transpose(2, 0, 1).reshape(-1)
    order = (np.arange(ROWS)[:, None] + ROWS * block[None, :]).reshape(-1)
    c, s = cosine[order], sine[order]
    return np.block([[c, s], [-s, c]])


def nn(a, b):
    return jnp.dot(a, b, preferred_element_type=F32)


def nt(a, b):
    return lax.dot_general(a, b, (((1,), (1,)), ((), ())), preferred_element_type=F32)


def iota(shape, axis):
    return lax.broadcasted_iota(I32, shape, axis)


def kernel(
    dims,
    scale,
    b_hbm,
    m_hbm,
    v_hbm,
    l_hbm,
    d_hbm,
    t_hbm,
    grad_hbm,
    fg_hbm,
    bv,
    mv,
    lv,
    dv,
    t_ref,
    bf,
    mf,
    lt,
    kt,
    img,
    ht,
    hn,
    mix,
    pb,
    vbt,
    vc,
    ph,
    rowid,
    perm,
    permt,
    sx,
    xr,
    sy,
    yr,
    sz,
    zr,
    ra,
    lg,
    vg,
    kg,
    kd,
    ea,
    zg,
    gv,
    gout,
    gs,
    gz,
    gt,
    gx,
    fo,
    local,
    send,
    rx,
    ry,
    rz,
    ray,
    rax,
    slx,
    rlx,
    rlc,
    rv,
    rk,
    sgz,
    rgz,
    sgx,
    rgx,
):
    na, nb, nc, nf, chunks = dims
    coils = chunks * GROUP
    rank = b_hbm.shape[0] // 2
    slab, width = b_hbm.shape[1:]
    span = v_hbm.shape[1]
    frames = span * nf
    nab = na * nb
    blocks = nab * nc
    depth = slab * blocks
    cells = depth * ROWS
    me = lax.axis_index("cuts")
    fr = lax.axis_index("frame")
    ia, ib, ic = me // (nb * nc), (me // nc) % nb, me % nc
    ab = ia * nb + ib
    lane = 2 * frames
    sl = slab * rank
    mesh_id = pl.DeviceIdType.MESH

    def cut(a, b, c):
        return a * (nb * nc) + b * nc + c

    def peer_a(j):
        return {"cuts": cut(lax.rem(ia + j, na), ib, ic)}

    def peer_b(j):
        return {"cuts": cut(ia, lax.rem(ib + j, nb), ic)}

    def peer_c(j):
        return {"cuts": cut(ia, ib, lax.rem(ic + j, nc))}

    def peer_f(j):
        return {"frame": lax.rem(fr + j, nf)}

    def peer_ab(j):
        return {"cuts": cut(lax.rem(ia + j // nb, na), lax.rem(ib + j % nb, nb), ic)}

    def peer_cf(j):
        return {
            "cuts": cut(ia, ib, lax.rem(ic + j // nf, nc)),
            "frame": lax.rem(fr + j % nf, nf),
        }

    def remote(src, dst, s, r, who):
        return pltpu.make_async_remote_copy(
            src_ref=src, dst_ref=dst, send_sem=s, recv_sem=r, device_id=who, device_id_type=mesh_id
        )

    everyone = [peer_ab(j) for j in range(1, nab)] + [peer_cf(j) for j in range(1, nc * nf)]
    barrier = pltpu.get_barrier_semaphore()
    for who in everyone:
        pl.semaphore_signal(barrier, inc=1, device_id=who, device_id_type=mesh_id)

    loads = [
        pltpu.make_async_copy(l_hbm, lv, local.at[0]),
        pltpu.make_async_copy(b_hbm, bv, local.at[1]),
        pltpu.make_async_copy(m_hbm, mv, local.at[2]),
        pltpu.make_async_copy(t_hbm, t_ref, local.at[3]),
        pltpu.make_async_copy(v_hbm, vg.at[fr], local.at[4]),
        pltpu.make_async_copy(d_hbm, dv, local.at[5]),
    ]
    for copy in loads:
        copy.start()

    n_rows = GROUP * blocks
    out_row = iota((n_rows, n_rows), 0)
    in_row = iota((n_rows, n_rows), 1)

    def spot(r):
        return r // nc % GROUP * blocks + r % nc * nab + r // (nc * GROUP)

    perm[...] = (spot(out_row) == in_row).astype(F32).astype(BF)
    permt[...] = (spot(in_row) == out_row).astype(F32).astype(BF)

    loads[0].wait()
    row = lv[0:1, :] + lv[1:2, :] * cells
    lt[0:1, 0:frames] = row
    lt[0:1, frames:lane] = row
    lg[ic, pl.ds(ab, 1)] = lt[...][None]
    loads[1].wait()
    loads[2].wait()
    for p in range(2):
        x = bv[p * rank : (p + 1) * rank].astype(F32)
        for z in range(slab):
            bf[z, p] = x[:, z, :]
    mf[...] = mv[...].astype(F32)
    loads[3].wait()
    loads[4].wait()

    def forward(k, carry):
        for c4 in range(GROUP):
            c = k * GROUP + c4
            for z in range(slab):
                mr, mi = mf[c, z : z + 1, :], mf[coils + c, z : z + 1, :]
                br, bi = bf[z, 0], bf[z, 1]
                at = (c4 * slab + z) * rank
                img[k, at : at + rank, 0:width] = (mr * br - mi * bi).astype(BF)
                img[k, at : at + rank, width : 2 * width] = (mr * bi + mi * br).astype(BF)
        ht[k] = nt(t_ref[...], img[k]).astype(BF)
        return carry

    pl.semaphore_wait(barrier, len(everyone))

    lab = [
        remote(
            lg.at[ic, pl.ds(ab, 1)], lg.at[ic, pl.ds(ab, 1)], slx.at[j], rlx.at[j], peer_ab(j)
        )
        for j in range(1, nab)
    ]
    vcopies = [
        remote(vg.at[fr], vg.at[fr], send.at[0, j], rv.at[j], peer_f(j)) for j in range(1, nf)
    ]
    for copy in lab + vcopies:
        copy.start()
    lax.fori_loop(0, chunks, forward, 0)

    def again(k, carry):
        full = nt(img[k], t_ref[...]).astype(BF)
        for c4 in range(GROUP):
            hn[k, c4, 0:sl, :] = full[c4 * sl : (c4 + 1) * sl, 0:width]
            hn[k, c4, sl : 2 * sl, :] = full[c4 * sl : (c4 + 1) * sl, width : 2 * width]
        return carry

    lax.fori_loop(0, chunks, again, 0)
    loads[5].wait()
    kt[...] = jnp.zeros_like(kt)
    for q in range(2):
        x = dv[q * coils : (q + 1) * coils].astype(F32)
        for s in range(2):
            kt[0:coils, q * lane + s * frames : q * lane + (s + 1) * frames] = x[:, s, :]
    kg[ic] = kt[...].astype(BF)
    kcopies = [
        remote(kg.at[ic], kg.at[ic], send.at[1, j], rk.at[j], peer_c(j)) for j in range(1, nc)
    ]
    for copy in lab:
        copy.wait()
    lc = [
        remote(lg.at[ic], lg.at[ic], send.at[2, j], rlc.at[j], peer_c(j)) for j in range(1, nc)
    ]
    for copy in lc + kcopies:
        copy.start()
    for copy in vcopies:
        copy.wait()

    vt = [vg[:, p].reshape(frames, rank) for p in range(2)]
    rep = (iota((rank, 4 * rank), 0) == iota((rank, 4 * rank), 1) % rank).astype(F32).astype(BF)
    wide = [nn(vt[p], rep) for p in range(2)]
    block_of = iota((frames, 4 * rank), 1) // rank
    for blk in range(4):
        r_ = jnp.where(block_of == blk, wide[0], 0.0).astype(BF)
        i_ = jnp.where(block_of == blk, wide[1], 0.0).astype(BF)
        at = blk * frames
        vbt[at : at + frames, 0 : 4 * rank] = r_
        vbt[at : at + frames, 4 * rank : 8 * rank] = -i_
        at = (4 + blk) * frames
        vbt[at : at + frames, 0 : 4 * rank] = i_
        vbt[at : at + frames, 4 * rank : 8 * rank] = r_
    rep2 = (iota((sl, rank), 0) % rank == iota((sl, rank), 1)).astype(F32).astype(BF)
    same = iota((sl, lane), 0) // rank == iota((sl, lane), 1) // frames
    tall = [nt(rep2, jnp.concatenate([vt[p], vt[p]], 0)) for p in range(2)]
    r_ = jnp.where(same, tall[0], 0.0).astype(BF)
    i_ = jnp.where(same, tall[1], 0.0).astype(BF)
    vc[0:sl, 0:lane] = r_
    vc[0:sl, lane : 2 * lane] = i_
    vc[sl : 2 * sl, 0:lane] = -i_
    vc[sl : 2 * sl, lane : 2 * lane] = r_

    def mixing(i, carry):
        k, pair = i // 2, i % 2
        for half in range(2):
            at = half * 2 * sl

            @pl.when(pair == half)
            def _():
                lhs = jnp.concatenate(
                    [ht[k, 0:width, at : at + 2 * sl], ht[k, width : 2 * width, at : at + 2 * sl]],
                    1,
                )
                mix[i] = nt(lhs, vbt[...])

        return carry

    lax.fori_loop(0, 2 * chunks, mixing, 0)
    for copy in kcopies:
        copy.wait()
    kall = kg[...].reshape(nc * 16, 2 * lane)
    krow = iota((chunks * GROUP * nc, nc * 16), 0)
    kcol = iota((chunks * GROUP * nc, nc * 16), 1)
    pick = (krow % nc * 16 + krow // nc == kcol).astype(F32).astype(BF)
    kd[...] = nn(pick, kall).reshape(chunks, GROUP * nc, 2 * lane)
    for copy in lc:
        copy.wait()

    lo = iota((blocks, lane), 1) < frames
    both = lg[...].reshape(blocks, lane)
    zpos = me * slab + iota((blocks, lane), 1) // frames
    norm = 1.0 / math.sqrt(depth)
    for s in range(2):
        mine = lax.rem(both, cells) if s == 0 else lax.div(both, cells)
        kz = lax.rem(mine, depth)
        rowid[s] = lax.div(mine, depth)
        angle = lax.rem(kz * zpos, depth).astype(F32) * (2.0 * math.pi / depth)
        ph[s, 0] = (jnp.cos(angle) * norm).astype(BF).astype(F32)
        ph[s, 1] = (jnp.sin(angle) * -norm).astype(BF).astype(F32)

    def to_a(k, j):
        return remote(
            sx.at[k, lax.rem(ia + j, na)], xr.at[k, j], send.at[5 + k, j], rx.at[k, j], peer_a(j)
        )

    def to_b(k, j):
        return remote(
            sy.at[k, lax.rem(ib + j, nb)], yr.at[k, j], send.at[8 + k, j], ry.at[k, j], peer_b(j)
        )

    def to_c(k, j):
        return remote(sz.at[k], zr.at[k, j], send.at[11 + k, j], rz.at[k, j], peer_c(j))

    def back_b(k, j):
        return remote(
            ra.at[k, ia, ib], ra.at[k, ia, ib], send.at[14 + k, j], ray.at[k, j], peer_b(j)
        )

    def back_a(k, j):
        return remote(ra.at[k, ia], ra.at[k, ia], send.at[17 + k, j], rax.at[k, j], peer_a(j))

    def parts_of(k, carry):
        for c4 in range(GROUP):
            i, c2 = k * 2 + c4 // 2, c4 % 2
            re0, im0 = c2 * lane, (2 + c2) * lane
            got = []
            for s in range(2):
                rs = rowid[s]
                mr = mix[i, 0:blocks, re0 : re0 + lane]
                mi = mix[i, 0:blocks, im0 : im0 + lane]
                for r in range(1, ROWS):
                    here = rs == r
                    mr = jnp.where(here, mix[i, r * blocks : (r + 1) * blocks, re0 : re0 + lane], mr)
                    mi = jnp.where(here, mix[i, r * blocks : (r + 1) * blocks, im0 : im0 + lane], mi)
                pr, pi = ph[s, 0], ph[s, 1]
                got.append((pr * mr - pi * mi, pr * mi + pi * mr))
            row = c4 * blocks
            for q in range(2):
                keep = jnp.where(lo, got[0][q], got[1][q])
                fold = jnp.where(lo, got[1][q], got[0][q])
                total = keep + pltpu.roll(fold, frames, 1)
                pb[row : row + blocks, q * lane : (q + 1) * lane] = total.astype(BF)
        part = nn(perm[...], pb[...]).astype(BF)
        sx[k] = part.reshape(na, nb, GROUP * nc, 2 * lane)
        for j in range(1, na):
            to_a(k, j).start()
        return carry

    lax.fori_loop(0, chunks, parts_of, 0)

    for k in range(chunks):
        total = sx[k, ia].astype(F32)
        for j in range(1, na):
            to_a(k, j).wait()
            total = total + xr[k, j].astype(F32)
        sy[k] = total.astype(BF)
        for j in range(1, nb):
            to_b(k, j).start()
    for k in range(chunks):
        total = sy[k, ib].astype(F32)
        for j in range(1, nb):
            to_b(k, j).wait()
            total = total + yr[k, j].astype(F32)
        sz[k] = total.astype(BF)
        for j in range(1, nc):
            to_c(k, j).start()
    for k in range(chunks):
        total = sz[k].astype(F32)
        for j in range(1, nc):
            to_c(k, j).wait()
            total = total + zr[k, j].astype(F32)
        ra[k, ia, ib] = (total - kd[k]).astype(BF)
        for j in range(1, nb):
            back_b(k, j).start()
    for k in range(chunks):
        for j in range(1, nb):
            back_b(k, j).wait()
        for j in range(1, na):
            back_a(k, j).start()
    gv[...] = jnp.zeros_like(gv)

    def spread(k, carry):
        for j in range(1, na):
            back_a(k, j).wait()
        resid = nn(permt[...], ra[k].reshape(n_rows, 2 * lane))
        for c4 in range(GROUP):
            here = [
                resid[c4 * blocks : (c4 + 1) * blocks, q * lane : (q + 1) * lane] for q in range(2)
            ]
            flip = [pltpu.roll(x, frames, 1) for x in here]
            terms = []
            for s in range(2):
                xr_, xi_ = [
                    jnp.where(lo, a, b) if s == 0 else jnp.where(lo, b, a)
                    for a, b in zip(here, flip)
                ]
                pr, pi = ph[s, 0], ph[s, 1]
                terms.append((xr_ * pr + xi_ * pi, xi_ * pr - xr_ * pi))
            for r in range(ROWS):
                m0, m1 = rowid[0] == r, rowid[1] == r
                for q in range(2):
                    ea[k, c4, r * blocks : (r + 1) * blocks, q * lane : (q + 1) * lane] = (
                        jnp.where(m0, terms[0][q], 0.0) + jnp.where(m1, terms[1][q], 0.0)
                    ).astype(BF)
            gv[...] += nn(hn[k, c4], ea[k, c4])
        return carry

    lax.fori_loop(0, chunks, spread, 0)

    own = {}
    for p in range(2):
        for q in range(2):
            first = gv[p * sl : p * sl + rank, q * lane : (q + 1) * lane]
            second = gv[p * sl + rank : (p + 1) * sl, q * lane : (q + 1) * lane]
            own[p, q] = first + pltpu.roll(second, frames, 1)
    gre = (own[0, 0] + own[1, 1]) * scale
    gim = (own[0, 1] - own[1, 0]) * scale
    turned = jnp.transpose(jnp.concatenate([gre, gim, gre, gim], 0))
    half = span // 2
    first_half = iota((half, 4 * rank), 1) < 2 * rank
    for f in range(nf):
        gs[f] = jnp.where(
            first_half,
            turned[f * span : f * span + half],
            turned[f * span + half : (f + 1) * span],
        ).astype(BF)
    gcf = [
        remote(gs.at[lax.rem(fr + j % nf, nf)], gz.at[j], sgz.at[j], rgz.at[j], peer_cf(j))
        for j in range(1, nc * nf)
    ]
    for copy in gcf:
        copy.start()

    def backward(k, carry):
        for c4 in range(GROUP):
            zc = nt(vc[...], ea[k, c4]).astype(BF)
            zg[k, c4 * sl : (c4 + 1) * sl, 0:width] = zc[0:sl]
            zg[k, c4 * sl : (c4 + 1) * sl, width : 2 * width] = zc[sl : 2 * sl]
        back = nn(zg[k], t_ref[...])
        out = list(carry)
        for z in range(slab):
            re, im = out[2 * z], out[2 * z + 1]
            for c4 in range(GROUP):
                c = k * GROUP + c4
                mr, mi = mf[c, z : z + 1, :], mf[coils + c, z : z + 1, :]
                at = (c4 * slab + z) * rank
                br = back[at : at + rank, 0:width]
                bi = back[at : at + rank, width : 2 * width]
                re = re + mr * br + mi * bi
                im = im + mr * bi - mi * br
            out[2 * z], out[2 * z + 1] = re, im
        return tuple(out)

    zero = jnp.zeros((rank, width), F32)
    out = lax.fori_loop(0, chunks, backward, (zero,) * (2 * slab))
    for z in range(slab):
        for p in range(2):
            gout[p * rank : (p + 1) * rank, z] = out[2 * z + p].reshape(rank, 1, width)
    store = pltpu.make_async_copy(gout, grad_hbm, local.at[6])
    store.start()

    total = gs[fr].astype(F32)
    for j, copy in enumerate(gcf):
        copy.wait()
        total = total + gz[j + 1].astype(F32)
    gt[...] = total
    gab = [remote(gt, gx.at[j], sgx.at[j], rgx.at[j], peer_ab(j)) for j in range(1, nab)]
    for copy in gab:
        copy.start()
    for j, copy in enumerate(gab):
        copy.wait()
        total = total + gx[j + 1]
    for q in range(2):
        for h in range(2):
            at = (2 * h + q) * rank
            fo[q, h * half : (h + 1) * half, :] = total[:, at : at + rank]
    last = pltpu.make_async_copy(fo, fg_hbm, local.at[7])
    last.start()
    last.wait()
    store.wait()


SHAPES = {64: (4, 4, 4), 8: (2, 2, 2)}


def body(basis, coil_maps, factors, lines, kdata):
    n_cuts = lax.axis_size("cuts")
    nf = lax.axis_size("frame")
    na, nb, nc = SHAPES[n_cuts]
    rank, slab, width = basis.shape[1], basis.shape[2], basis.shape[4]
    coils = coil_maps.shape[1]
    chunks = coils // GROUP
    span = factors.shape[2]
    lpd = lines.shape[1]
    frames = span * nf
    lane = 2 * frames
    sl = slab * rank
    blocks = n_cuts
    n_rows = GROUP * blocks
    scale = 1.0 / math.sqrt(coils * lpd * n_cuts * basis.shape[3] * nf)
    table = jnp.asarray(real_table(width, (na, nb, nc)), BF)
    b = basis.transpose(0, 1, 3, 2, 4).reshape(2 * rank, slab, width)
    m = coil_maps.transpose(0, 1, 3, 2, 4).reshape(2 * coils, slab, width)
    v = factors.transpose(0, 2, 1)
    l = lines.T
    d = kdata.transpose(0, 3, 4, 2, 1).reshape(2 * coils, lpd, frames)
    dma = pltpu.SemaphoreType.DMA
    vm = pltpu.VMEM
    slabs = (chunks, na, nb, GROUP * nc, 2 * lane)
    scratch = [
        vm(b.shape, BF),
        vm(m.shape, BF),
        vm(l.shape, I32),
        vm(d.shape, BF),
        vm(table.shape, BF),
        vm((slab, 2, rank, width), F32),
        vm(m.shape, F32),
        vm((1, lane), I32),
        vm((16, 2 * lane), F32),
        vm((chunks, GROUP * sl, 2 * width), BF),
        vm((chunks, 2 * width, GROUP * sl), BF),
        vm((chunks, GROUP, 2 * sl, width), BF),
        vm((2 * chunks, width, 4 * lane), F32),
        vm((n_rows, 2 * lane), BF),
        vm((8 * frames, 8 * rank), BF),
        vm((2 * sl, 2 * lane), BF),
        vm((2, 2, blocks, lane), F32),
        vm((2, blocks, lane), I32),
        vm((n_rows, n_rows), BF),
        vm((n_rows, n_rows), BF),
        vm(slabs, BF),
        vm((chunks, na) + slabs[2:], BF),
        vm((chunks,) + slabs[2:], BF),
        vm((chunks,) + slabs[2:], BF),
        vm((chunks,) + slabs[3:], BF),
        vm((chunks, nc) + slabs[3:], BF),
        vm(slabs, BF),
        vm((nc, na * nb, 1, lane), I32),
        vm((nf, 2, span, rank), BF),
        vm((nc, 16, 2 * lane), BF),
        vm((chunks,) + slabs[3:], F32),
        vm((chunks, GROUP, width, 2 * lane), BF),
        vm((chunks, GROUP * sl, 2 * width), BF),
        vm((2 * sl, 2 * lane), F32),
        vm((2 * rank, slab, 1, width), F32),
        vm((nf, span // 2, 4 * rank), BF),
        vm((nc * nf, span // 2, 4 * rank), BF),
        vm((span // 2, 4 * rank), F32),
        vm((na * nb, span // 2, 4 * rank), F32),
        vm((2, span, rank), F32),
        dma((8,)),
        dma((20, 4)),
        dma((3, 4)),
        dma((3, 4)),
        dma((3, 4)),
        dma((3, 4)),
        dma((3, 4)),
        dma((na * nb,)),
        dma((na * nb,)),
        dma((4,)),
        dma((4,)),
        dma((4,)),
        dma((nc * nf,)),
        dma((nc * nf,)),
        dma((na * nb,)),
        dma((na * nb,)),
    ]
    grad, fg = pl.pallas_call(
        functools.partial(kernel, (na, nb, nc, nf, chunks), scale),
        out_shape=(
            jax.ShapeDtypeStruct((2 * rank, slab, 1, width), F32),
            jax.ShapeDtypeStruct((2, span, rank), F32),
        ),
        in_specs=[pl.BlockSpec(memory_space=pl.ANY)] * 6,
        out_specs=[pl.BlockSpec(memory_space=pl.ANY)] * 2,
        scratch_shapes=scratch,
        compiler_params=pltpu.CompilerParams(
            collective_id=0, has_side_effects=True, vmem_limit_bytes=56 * 1024 * 1024
        ),
    )(b, m, v, l, d, table)
    return grad.reshape(basis.shape), fg.transpose(0, 2, 1)


def solution(mesh):
    placed = (
        P(None, None, "cuts", "frame", None),
        P(None, None, "cuts", "frame", None),
        P(None, None, "frame"),
        P(None, "cuts"),
        P(None, None, "cuts", None, "frame"),
    )
    return jax.shard_map(
        body,
        mesh=mesh,
        in_specs=placed,
        out_specs=(P(None, None, "cuts", "frame", None), P(None, None, "frame")),
        check_vma=False,
    )
```

```python
import functools
import math

import jax
import jax.numpy as jnp
import numpy as np
from jax import lax
from jax.experimental import pallas as pl
from jax.experimental.pallas import tpu as pltpu
from jax.sharding import PartitionSpec as P

BF = jnp.bfloat16
F32 = jnp.float32
I32 = jnp.int32
GROUP = 4
ROWS = 4


def real_table(size, shape):
    index = np.arange(size)
    angle = (index[:, None] * index[None, :] % size) * (2.0 * math.pi / size)
    cosine, sine = np.cos(angle) / math.sqrt(size), np.sin(angle) / math.sqrt(size)
    whole = np.stack([np.concatenate([cosine, sine], 1), np.concatenate([-sine, cosine], 1)])
    whole = whole.reshape((2,) + tuple(shape) + (ROWS, 2 * size))
    first = whole.transpose(1, 2, 0, 4, 3, 5).reshape(2 * size, 2 * size)
    second = whole.transpose(0, 4, 3, 1, 2, 5).reshape(2 * size, 2 * size)
    return first, second


def nn(a, b):
    return jnp.dot(a, b, preferred_element_type=F32)


def nt(a, b):
    return lax.dot_general(a, b, (((1,), (1,)), ((), ())), preferred_element_type=F32)


def iota(shape, axis):
    return lax.broadcasted_iota(I32, shape, axis)


def kernel(
    dims,
    scale,
    b_hbm,
    m_hbm,
    v_hbm,
    l_hbm,
    d_hbm,
    t_hbm,
    t2_hbm,
    grad_hbm,
    fg_hbm,
    bv,
    mv,
    lv,
    dv,
    t_ref,
    t2_ref,
    bf,
    mf,
    lt,
    l8,
    kt,
    img,
    ht,
    hr,
    hn,
    vbt,
    vc,
    pf,
    ph,
    rowid,
    permt,
    zr,
    ra,
    lg,
    vg,
    kg,
    kd,
    ea,
    zg,
    gv,
    gout,
    gs,
    gz,
    gx,
    fo,
    local,
    send,
    recv,
):
    na, nb, nc, nf, chunks = dims
    coils = chunks * GROUP
    rank = b_hbm.shape[0] // 2
    slab, width = b_hbm.shape[1:]
    span = v_hbm.shape[1]
    frames = span * nf
    nab = na * nb
    blocks = nab * nc
    depth = slab * blocks
    cells = depth * ROWS
    me = lax.axis_index("cuts")
    fr = lax.axis_index("frame")
    ia, ib, ic = me // (nb * nc), (me // nc) % nb, me % nc
    ab = ia * nb + ib
    lane = 2 * frames
    sl = slab * rank
    mesh_id = pl.DeviceIdType.MESH

    def cut(a, b, c):
        return a * (nb * nc) + b * nc + c

    def peer_c(j):
        return {"cuts": cut(ia, ib, lax.rem(ic + j, nc))}

    def peer_f(j):
        return {"frame": lax.rem(fr + j, nf)}

    def peer_ab(j):
        return {"cuts": cut(lax.rem(ia + j // nb, na), lax.rem(ib + j % nb, nb), ic)}

    def peer_cf(j):
        return {
            "cuts": cut(ia, ib, lax.rem(ic + j // nf, nc)),
            "frame": lax.rem(fr + j % nf, nf),
        }

    def remote(src, dst, s, r, who):
        return pltpu.make_async_remote_copy(
            src_ref=src, dst_ref=dst, send_sem=s, recv_sem=r, device_id=who, device_id_type=mesh_id
        )

    everyone = [peer_ab(j) for j in range(1, nab)] + [peer_cf(j) for j in range(1, nc * nf)]
    barrier = pltpu.get_barrier_semaphore()
    for who in everyone:
        pl.semaphore_signal(barrier, inc=1, device_id=who, device_id_type=mesh_id)

    def settle(block, at):
        pltpu.make_async_copy(block, block, send.at[at]).wait()
        pltpu.make_async_copy(block, block, recv.at[at]).wait()

    loads = [
        pltpu.make_async_copy(l_hbm, lv, local.at[0]),
        pltpu.make_async_copy(b_hbm, bv, local.at[1]),
        pltpu.make_async_copy(m_hbm, mv, local.at[2]),
        pltpu.make_async_copy(t_hbm, t_ref, local.at[3]),
        pltpu.make_async_copy(v_hbm, vg.at[fr], local.at[4]),
        pltpu.make_async_copy(d_hbm, dv, local.at[5]),
        pltpu.make_async_copy(t2_hbm, t2_ref, local.at[6]),
    ]
    for copy in loads:
        copy.start()
    loads[0].wait()
    row = lv[0:1, :] + lv[1:2, :] * cells
    lt[0:1, 0:frames] = row
    lt[0:1, frames:lane] = row
    lg[ic, pl.ds(ab, 1)] = lt[...][None]
    loads[1].wait()
    loads[2].wait()
    for p in range(2):
        x = bv[p * rank : (p + 1) * rank].astype(F32)
        for z in range(slab):
            bf[z, p] = x[:, z, :]
    mf[...] = mv[...].astype(F32)
    loads[3].wait()
    loads[4].wait()

    def forward(k, carry):
        for c4 in range(GROUP):
            c = k * GROUP + c4
            for z in range(slab):
                mr, mi = mf[c, z : z + 1, :], mf[coils + c, z : z + 1, :]
                br, bi = bf[z, 0], bf[z, 1]
                at = (c4 * slab + z) * rank
                img[k, at : at + rank, 0:width] = (mr * br - mi * bi).astype(BF)
                img[k, at : at + rank, width : 2 * width] = (mr * bi + mi * br).astype(BF)
        ht[k] = nt(t_ref[...], img[k]).astype(BF).reshape(nab, 2, ROWS * nc, GROUP * sl)
        hr[k, ab] = ht[k, ab]
        return carry

    lax.fori_loop(0, chunks, forward, 0)

    pl.semaphore_wait(barrier, len(everyone))

    for j in range(1, nc):
        own_line = lg.at[ic, pl.ds(ab, 1)]
        remote(own_line, own_line, send.at[0], recv.at[0], peer_c(j)).start()
    for k in range(chunks):
        for j in range(1, nab):
            to = lax.rem(ia + j // nb, na) * nb + lax.rem(ib + j % nb, nb)
            remote(
                ht.at[k, to], hr.at[k, ab], send.at[1 + k], recv.at[1 + k], peer_ab(j)
            ).start()
    for j in range(1, nf):
        remote(vg.at[fr], vg.at[fr], send.at[4], recv.at[4], peer_f(j)).start()
    loads[5].wait()
    kt[...] = jnp.zeros_like(kt)
    for q in range(2):
        x = dv[q * coils : (q + 1) * coils].astype(F32)
        for s in range(2):
            kt[0:coils, q * lane + s * frames : q * lane + (s + 1) * frames] = x[:, s, :]
    kg[ic] = kt[...].astype(BF)
    for j in range(1, nc):
        remote(kg.at[ic], kg.at[ic], send.at[5], recv.at[5], peer_c(j)).start()
    loads[6].wait()

    def again(k, carry):
        full = nt(img[k], t2_ref[...]).astype(BF)
        for c4 in range(GROUP):
            hn[k, c4, 0:sl, :] = full[c4 * sl : (c4 + 1) * sl, 0:width]
            hn[k, c4, sl : 2 * sl, :] = full[c4 * sl : (c4 + 1) * sl, width : 2 * width]
        return carry

    lax.fori_loop(0, chunks, again, 0)
    settle(lg.at[pl.ds(0, nc - 1), pl.ds(0, 1)], 0)
    for j in range(1, nab):
        mine = lg.at[:, pl.ds(ab, 1)]
        remote(mine, mine, send.at[6], recv.at[6], peer_ab(j)).start()
    pair_rows = 2 * nc
    l8[0:nc] = lg[:, ab]
    l8[nc:pair_rows] = lg[:, ab]
    both = l8[...].reshape(pair_rows, lane)
    norm = 1.0 / math.sqrt(depth)
    odd = iota((pair_rows, lane), 0) // nc
    zlane = iota((pair_rows, lane), 1) // frames
    upper = []
    for s in range(2):
        mine = lax.rem(both, cells) if s == 0 else lax.div(both, cells)
        kz = lax.rem(mine, depth)
        r = lax.div(mine, depth)
        upper.append(r >= 2)
        here = lax.rem(r, 2) == odd
        for i in range(nab):
            zpos = (i * nc + ic) * slab + zlane
            angle = lax.rem(kz * zpos, depth).astype(F32) * (2.0 * math.pi / depth)
            pf[s, 0, i] = jnp.where(here, (jnp.cos(angle) * norm).astype(BF).astype(F32), 0.0)
            pf[s, 1, i] = jnp.where(here, (jnp.sin(angle) * -norm).astype(BF).astype(F32), 0.0)
    settle(vg.at[pl.ds(0, nf - 1)], 4)

    vt = [vg[:, p].reshape(frames, rank) for p in range(2)]
    rep = (iota((rank, 4 * rank), 0) == iota((rank, 4 * rank), 1) % rank).astype(F32).astype(BF)
    wide = [nn(vt[p], rep) for p in range(2)]
    block_of = iota((frames, 4 * rank), 1) // rank
    for blk in range(4):
        r_ = jnp.where(block_of == blk, wide[0], 0.0).astype(BF)
        i_ = jnp.where(block_of == blk, wide[1], 0.0).astype(BF)
        at = blk * frames
        vbt[at : at + frames, 0 : 4 * rank] = r_
        vbt[at : at + frames, 4 * rank : 8 * rank] = -i_
        at = (4 + blk) * frames
        vbt[at : at + frames, 0 : 4 * rank] = i_
        vbt[at : at + frames, 4 * rank : 8 * rank] = r_
    rep2 = (iota((sl, rank), 0) % rank == iota((sl, rank), 1)).astype(F32).astype(BF)
    same = iota((sl, lane), 0) // rank == iota((sl, lane), 1) // frames
    tall = [nt(rep2, jnp.concatenate([vt[p], vt[p]], 0)) for p in range(2)]
    r_ = jnp.where(same, tall[0], 0.0).astype(BF)
    i_ = jnp.where(same, tall[1], 0.0).astype(BF)
    vc[0:sl, 0:lane] = r_
    vc[0:sl, lane : 2 * lane] = i_
    vc[sl : 2 * sl, 0:lane] = -i_
    vc[sl : 2 * sl, lane : 2 * lane] = r_
    n_rows = GROUP * blocks
    out_row = iota((n_rows, n_rows), 0)
    in_row = iota((n_rows, n_rows), 1)
    spot = in_row // nc % GROUP * blocks + in_row % nc * nab + in_row // (nc * GROUP)
    permt[...] = (spot == out_row).astype(F32).astype(BF)
    settle(kg.at[pl.ds(0, nc - 1)], 5)
    kall = kg[...].reshape(nc * 16, 2 * lane)
    krow = iota((chunks * GROUP * nc, nc * 16), 0)
    kcol = iota((chunks * GROUP * nc, nc * 16), 1)
    pick = (krow % nc * 16 + krow // nc == kcol).astype(F32).astype(BF)
    kd[...] = nn(pick, kall).reshape(chunks, GROUP * nc, 2 * lane)
    lo8 = iota((pair_rows, lane), 1) < frames
    top = iota((pair_rows, lane), 0) < nc

    def parts_of(k, carry):
        settle(hr.at[k, pl.ds(0, nab - 1)], 1 + k)
        tiles = []
        for pair in range(GROUP // 2):
            at = pair * 2 * sl
            lhs = jnp.concatenate(
                [hr[k, :, p, :, at : at + 2 * sl].reshape(width, 2 * sl) for p in range(2)], 1
            )
            mixed = nt(lhs, vbt[...]).reshape(nab, ROWS * nc, 4 * lane)
            totals = []
            for c2 in range(2):
                re0, im0 = c2 * lane, (2 + c2) * lane
                got = []
                for s in range(2):
                    mr = jnp.where(
                        upper[s][None],
                        mixed[:, pair_rows:, re0 : re0 + lane],
                        mixed[:, :pair_rows, re0 : re0 + lane],
                    )
                    mi = jnp.where(
                        upper[s][None],
                        mixed[:, pair_rows:, im0 : im0 + lane],
                        mixed[:, :pair_rows, im0 : im0 + lane],
                    )
                    pr, pi = pf[s, 0], pf[s, 1]
                    got.append((jnp.sum(pr * mr - pi * mi, 0), jnp.sum(pr * mi + pi * mr, 0)))
                both_q = []
                for q in range(2):
                    keep = jnp.where(lo8, got[0][q], got[1][q])
                    fold = jnp.where(lo8, got[1][q], got[0][q])
                    total = keep + pltpu.roll(fold, frames, 1)
                    both_q.append(total + pltpu.roll(total, nc, 0))
                totals.append(both_q)
            tiles.append(
                jnp.concatenate([jnp.where(top, totals[0][q], totals[1][q]) for q in range(2)], 1)
            )
        zr[k, ic] = jnp.concatenate(tiles, 0).astype(BF)
        for j in range(1, nc):
            remote(
                zr.at[k, ic], zr.at[k, ic], send.at[7 + k], recv.at[7 + k], peer_c(j)
            ).start()
        return carry

    lax.fori_loop(0, chunks, parts_of, 0)
    settle(lg.at[:, pl.ds(0, nab - 1)], 6)
    lo = iota((blocks, lane), 1) < frames
    both = lg[...].reshape(blocks, lane)
    zpos = me * slab + iota((blocks, lane), 1) // frames
    for s in range(2):
        mine = lax.rem(both, cells) if s == 0 else lax.div(both, cells)
        kz = lax.rem(mine, depth)
        rowid[s] = lax.div(mine, depth)
        angle = lax.rem(kz * zpos, depth).astype(F32) * (2.0 * math.pi / depth)
        ph[s, 0] = (jnp.cos(angle) * norm).astype(BF).astype(F32)
        ph[s, 1] = (jnp.sin(angle) * -norm).astype(BF).astype(F32)
    for k in range(chunks):
        settle(zr.at[k, pl.ds(0, nc - 1)], 7 + k)
        total = zr[k, 0].astype(F32)
        for j in range(1, nc):
            total = total + zr[k, j].astype(F32)
        ra[k, ab] = (total - kd[k]).astype(BF)
        for j in range(1, nab):
            remote(
                ra.at[k, ab], ra.at[k, ab], send.at[10 + k], recv.at[10 + k], peer_ab(j)
            ).start()
    gv[...] = jnp.zeros_like(gv)

    def spread(k, carry):
        settle(ra.at[k, pl.ds(0, nab - 1)], 10 + k)
        resid = nn(permt[...], ra[k].reshape(n_rows, 2 * lane))
        for c4 in range(GROUP):
            here = [
                resid[c4 * blocks : (c4 + 1) * blocks, q * lane : (q + 1) * lane] for q in range(2)
            ]
            flip = [pltpu.roll(x, frames, 1) for x in here]
            terms = []
            for s in range(2):
                xr_, xi_ = [
                    jnp.where(lo, a, b) if s == 0 else jnp.where(lo, b, a)
                    for a, b in zip(here, flip)
                ]
                pr, pi = ph[s, 0], ph[s, 1]
                terms.append((xr_ * pr + xi_ * pi, xi_ * pr - xr_ * pi))
            for r in range(ROWS):
                m0, m1 = rowid[0] == r, rowid[1] == r
                for q in range(2):
                    ea[k, c4, r * blocks : (r + 1) * blocks, q * lane : (q + 1) * lane] = (
                        jnp.where(m0, terms[0][q], 0.0) + jnp.where(m1, terms[1][q], 0.0)
                    ).astype(BF)
            gv[...] += nn(hn[k, c4], ea[k, c4])
        return carry

    lax.fori_loop(0, chunks, spread, 0)

    own = {}
    for p in range(2):
        for q in range(2):
            first = gv[p * sl : p * sl + rank, q * lane : (q + 1) * lane]
            second = gv[p * sl + rank : (p + 1) * sl, q * lane : (q + 1) * lane]
            own[p, q] = first + pltpu.roll(second, frames, 1)
    gre = (own[0, 0] + own[1, 1]) * scale
    gim = (own[0, 1] - own[1, 0]) * scale
    turned = jnp.transpose(jnp.concatenate([gre, gim, gre, gim], 0))
    half = span // 2
    first_half = iota((half, 4 * rank), 1) < 2 * rank
    for f in range(nf):
        gs[f] = jnp.where(
            first_half,
            turned[f * span : f * span + half],
            turned[f * span + half : (f + 1) * span],
        ).astype(BF)
    spot_cf = ic * nf + fr
    gz[spot_cf] = gs[fr]
    for j in range(1, nc * nf):
        remote(
            gs.at[lax.rem(fr + j % nf, nf)], gz.at[spot_cf], send.at[13], recv.at[13], peer_cf(j)
        ).start()

    def backward(k, carry):
        for c4 in range(GROUP):
            zc = nt(vc[...], ea[k, c4]).astype(BF)
            zg[k, c4 * sl : (c4 + 1) * sl, 0:width] = zc[0:sl]
            zg[k, c4 * sl : (c4 + 1) * sl, width : 2 * width] = zc[sl : 2 * sl]
        back = nn(zg[k], t2_ref[...])
        out = list(carry)
        for z in range(slab):
            re, im = out[2 * z], out[2 * z + 1]
            for c4 in range(GROUP):
                c = k * GROUP + c4
                mr, mi = mf[c, z : z + 1, :], mf[coils + c, z : z + 1, :]
                at = (c4 * slab + z) * rank
                br = back[at : at + rank, 0:width]
                bi = back[at : at + rank, width : 2 * width]
                re = re + mr * br + mi * bi
                im = im + mr * bi - mi * br
            out[2 * z], out[2 * z + 1] = re, im
        return tuple(out)

    zero = jnp.zeros((rank, width), F32)
    out = lax.fori_loop(0, chunks, backward, (zero,) * (2 * slab))
    for z in range(slab):
        for p in range(2):
            gout[p * rank : (p + 1) * rank, z] = out[2 * z + p].reshape(rank, 1, width)
    store = pltpu.make_async_copy(gout, grad_hbm, local.at[7])
    store.start()

    settle(gz.at[pl.ds(0, nc * nf - 1)], 13)
    gx[ab] = jnp.sum(gz[...].astype(F32), 0)
    for j in range(1, nab):
        remote(gx.at[ab], gx.at[ab], send.at[14], recv.at[14], peer_ab(j)).start()
    settle(gx.at[pl.ds(0, nab - 1)], 14)
    total = jnp.sum(gx[...], 0)
    for q in range(2):
        for h in range(2):
            at = (2 * h + q) * rank
            fo[q, h * half : (h + 1) * half, :] = total[:, at : at + rank]
    last = pltpu.make_async_copy(fo, fg_hbm, local.at[8])
    last.start()
    last.wait()
    store.wait()


SHAPES = {64: (4, 4, 4), 8: (2, 2, 2)}


def body(basis, coil_maps, factors, lines, kdata):
    n_cuts = lax.axis_size("cuts")
    nf = lax.axis_size("frame")
    na, nb, nc = SHAPES[n_cuts]
    rank, slab, width = basis.shape[1], basis.shape[2], basis.shape[4]
    coils = coil_maps.shape[1]
    chunks = coils // GROUP
    span = factors.shape[2]
    lpd = lines.shape[1]
    frames = span * nf
    lane = 2 * frames
    sl = slab * rank
    blocks = n_cuts
    n_rows = GROUP * blocks
    scale = 1.0 / math.sqrt(coils * lpd * n_cuts * basis.shape[3] * nf)
    table, table2 = (jnp.asarray(x, BF) for x in real_table(width, (na, nb, nc)))
    b = basis.transpose(0, 1, 3, 2, 4).reshape(2 * rank, slab, width)
    m = coil_maps.transpose(0, 1, 3, 2, 4).reshape(2 * coils, slab, width)
    v = factors.transpose(0, 2, 1)
    l = lines.T
    d = kdata.transpose(0, 3, 4, 2, 1).reshape(2 * coils, lpd, frames)
    dma = pltpu.SemaphoreType.DMA
    vm = pltpu.VMEM
    nab = na * nb
    scratch = [
        vm(b.shape, BF),
        vm(m.shape, BF),
        vm(l.shape, I32),
        vm(d.shape, BF),
        vm(table.shape, BF),
        vm(table.shape, BF),
        vm((slab, 2, rank, width), F32),
        vm(m.shape, F32),
        vm((1, lane), I32),
        vm((2 * nc, 1, lane), I32),
        vm((16, 2 * lane), F32),
        vm((chunks, GROUP * sl, 2 * width), BF),
        vm((chunks, nab, 2, ROWS * nc, GROUP * sl), BF),
        vm((chunks, nab, 2, ROWS * nc, GROUP * sl), BF),
        vm((chunks, GROUP, 2 * sl, width), BF),
        vm((8 * frames, 8 * rank), BF),
        vm((2 * sl, 2 * lane), BF),
        vm((2, 2, nab, 2 * nc, lane), F32),
        vm((2, 2, blocks, lane), F32),
        vm((2, blocks, lane), I32),
        vm((n_rows, n_rows), BF),
        vm((chunks, nc, GROUP * nc, 2 * lane), BF),
        vm((chunks, nab, GROUP * nc, 2 * lane), BF),
        vm((nc, nab, 1, lane), I32),
        vm((nf, 2, span, rank), BF),
        vm((nc, 16, 2 * lane), BF),
        vm((chunks, GROUP * nc, 2 * lane), F32),
        vm((chunks, GROUP, width, 2 * lane), BF),
        vm((chunks, GROUP * sl, 2 * width), BF),
        vm((2 * sl, 2 * lane), F32),
        vm((2 * rank, slab, 1, width), F32),
        vm((nf, span // 2, 4 * rank), BF),
        vm((nc * nf, span // 2, 4 * rank), BF),
        vm((nab, span // 2, 4 * rank), F32),
        vm((2, span, rank), F32),
        dma((9,)),
        dma((15,)),
        dma((15,)),
    ]
    grad, fg = pl.pallas_call(
        functools.partial(kernel, (na, nb, nc, nf, chunks), scale),
        out_shape=(
            jax.ShapeDtypeStruct((2 * rank, slab, 1, width), F32),
            jax.ShapeDtypeStruct((2, span, rank), F32),
        ),
        in_specs=[pl.BlockSpec(memory_space=pl.ANY)] * 7,
        out_specs=[pl.BlockSpec(memory_space=pl.ANY)] * 2,
        scratch_shapes=scratch,
        compiler_params=pltpu.CompilerParams(
            collective_id=0, has_side_effects=True, vmem_limit_bytes=56 * 1024 * 1024
        ),
    )(b, m, v, l, d, table, table2)
    return grad.reshape(basis.shape), fg.transpose(0, 2, 1)


def solution(mesh):
    placed = (
        P(None, None, "cuts", "frame", None),
        P(None, None, "cuts", "frame", None),
        P(None, None, "frame"),
        P(None, "cuts"),
        P(None, None, "cuts", None, "frame"),
    )
    return jax.shard_map(
        body,
        mesh=mesh,
        in_specs=placed,
        out_specs=(P(None, None, "cuts", "frame", None), P(None, None, "frame")),
        check_vma=False,
    )
```

```python
import functools
import math

import jax
import jax.numpy as jnp
import numpy as np
from jax import lax
from jax.experimental import pallas as pl
from jax.experimental.pallas import tpu as pltpu
from jax.sharding import PartitionSpec as P

BF = jnp.bfloat16
F32 = jnp.float32
I32 = jnp.int32
GROUP = 4
ROWS = 4


def real_table(size, shape):
    index = np.arange(size)
    angle = (index[:, None] * index[None, :] % size) * (2.0 * math.pi / size)
    cosine, sine = np.cos(angle) / math.sqrt(size), np.sin(angle) / math.sqrt(size)
    whole = np.stack([np.concatenate([cosine, sine], 1), np.concatenate([-sine, cosine], 1)])
    whole = whole.reshape((2,) + tuple(shape) + (ROWS, 2 * size))
    first = whole.transpose(1, 2, 0, 4, 3, 5).reshape(2 * size, 2 * size)
    second = whole.transpose(0, 4, 3, 1, 2, 5).reshape(2 * size, 2 * size)
    return first, second


def nn(a, b):
    return jnp.dot(a, b, preferred_element_type=F32)


def nt(a, b):
    return lax.dot_general(a, b, (((1,), (1,)), ((), ())), preferred_element_type=F32)


def iota(shape, axis):
    return lax.broadcasted_iota(I32, shape, axis)


def kernel(
    dims,
    scale,
    b_hbm,
    m_hbm,
    v_hbm,
    l_hbm,
    d_hbm,
    t_hbm,
    t2_hbm,
    gout,
    fo,
    bv,
    mv,
    lv,
    dv,
    t_ref,
    t2_ref,
    bf,
    mf,
    lt,
    l8,
    kt,
    img,
    ht,
    hr,
    hn,
    vbt,
    vc,
    pf,
    ph,
    rowid,
    permt,
    zr,
    ra,
    lg,
    vg,
    kg,
    kd,
    ea,
    zg,
    gv,
    gs,
    gz,
    gx,
    local,
    send,
    recv,
):
    na, nb, nc, nf, chunks = dims
    coils = chunks * GROUP
    rank = b_hbm.shape[0] // 2
    slab, width = b_hbm.shape[1:]
    span = v_hbm.shape[1]
    frames = span * nf
    nab = na * nb
    blocks = nab * nc
    depth = slab * blocks
    cells = depth * ROWS
    me = lax.axis_index("cuts")
    fr = lax.axis_index("frame")
    ia, ib, ic = me // (nb * nc), (me // nc) % nb, me % nc
    ab = ia * nb + ib
    lane = 2 * frames
    sl = slab * rank
    mesh_id = pl.DeviceIdType.MESH

    def cut(a, b, c):
        return a * (nb * nc) + b * nc + c

    def peer_c(j):
        return {"cuts": cut(ia, ib, lax.rem(ic + j, nc))}

    def peer_f(j):
        return {"frame": lax.rem(fr + j, nf)}

    def peer_ab(j):
        return {"cuts": cut(lax.rem(ia + j // nb, na), lax.rem(ib + j % nb, nb), ic)}

    def peer_cf(j):
        return {
            "cuts": cut(ia, ib, lax.rem(ic + j // nf, nc)),
            "frame": lax.rem(fr + j % nf, nf),
        }

    def remote(src, dst, s, r, who):
        return pltpu.make_async_remote_copy(
            src_ref=src, dst_ref=dst, send_sem=s, recv_sem=r, device_id=who, device_id_type=mesh_id
        )

    def far(j):
        da, db = j // nb, j % nb
        da, db = min(da, na - da), min(db, nb - db)
        return (-da, -db, j)

    others = sorted(range(1, nab), key=far)
    everyone = [peer_ab(j) for j in others] + [peer_cf(j) for j in range(1, nc * nf)]
    barrier = pltpu.get_barrier_semaphore()
    for who in everyone:
        pl.semaphore_signal(barrier, inc=1, device_id=who, device_id_type=mesh_id)

    def settle(block, at):
        pltpu.make_async_copy(block, block, send.at[at]).wait()
        pltpu.make_async_copy(block, block, recv.at[at]).wait()

    loads = [
        pltpu.make_async_copy(l_hbm, lv, local.at[0]),
        pltpu.make_async_copy(b_hbm, bv, local.at[1]),
        pltpu.make_async_copy(m_hbm, mv, local.at[2]),
        pltpu.make_async_copy(t_hbm, t_ref, local.at[3]),
        pltpu.make_async_copy(v_hbm, vg.at[fr], local.at[4]),
        pltpu.make_async_copy(d_hbm, dv, local.at[5]),
        pltpu.make_async_copy(t2_hbm, t2_ref, local.at[6]),
    ]
    for copy in loads:
        copy.start()
    loads[0].wait()
    row = lv[0:1, :] + lv[1:2, :] * cells
    lt[0:1, 0:frames] = row
    lt[0:1, frames:lane] = row
    lg[ic, pl.ds(ab, 1)] = lt[...][None]
    loads[1].wait()
    loads[2].wait()
    for p in range(2):
        x = bv[p * rank : (p + 1) * rank].astype(F32)
        for z in range(slab):
            bf[z, p] = x[:, z, :]
    mf[...] = mv[...].astype(F32)
    loads[3].wait()
    loads[4].wait()

    def forward(k, carry):
        for c4 in range(GROUP):
            c = k * GROUP + c4
            for z in range(slab):
                mr, mi = mf[c, z : z + 1, :], mf[coils + c, z : z + 1, :]
                br, bi = bf[z, 0], bf[z, 1]
                at = (c4 * slab + z) * rank
                img[k, at : at + rank, 0:width] = (mr * br - mi * bi).astype(BF)
                img[k, at : at + rank, width : 2 * width] = (mr * bi + mi * br).astype(BF)
        ht[k] = nt(t_ref[...], img[k]).astype(BF).reshape(nab, 2, ROWS * nc, GROUP * sl)
        hr[k, ab] = ht[k, ab]
        return carry

    lax.fori_loop(0, chunks, forward, 0)

    pl.semaphore_wait(barrier, len(everyone))

    for j in range(1, nc):
        own_line = lg.at[ic, pl.ds(ab, 1)]
        remote(own_line, own_line, send.at[0], recv.at[0], peer_c(j)).start()
    for k in range(chunks):
        for j in others:
            to = lax.rem(ia + j // nb, na) * nb + lax.rem(ib + j % nb, nb)
            remote(
                ht.at[k, to], hr.at[k, ab], send.at[1 + k], recv.at[1 + k], peer_ab(j)
            ).start()
    for j in range(1, nf):
        remote(vg.at[fr], vg.at[fr], send.at[4], recv.at[4], peer_f(j)).start()
    loads[5].wait()
    kt[...] = jnp.zeros_like(kt)
    for q in range(2):
        x = dv[q * coils : (q + 1) * coils].astype(F32)
        for s in range(2):
            kt[0:coils, q * lane + s * frames : q * lane + (s + 1) * frames] = x[:, s, :]
    kg[ic] = kt[...].astype(BF)
    for j in range(1, nc):
        remote(kg.at[ic], kg.at[ic], send.at[5], recv.at[5], peer_c(j)).start()
    loads[6].wait()

    def again(k, carry):
        full = nt(img[k], t2_ref[...]).astype(BF)
        for c4 in range(GROUP):
            hn[k, c4, 0:sl, :] = full[c4 * sl : (c4 + 1) * sl, 0:width]
            hn[k, c4, sl : 2 * sl, :] = full[c4 * sl : (c4 + 1) * sl, width : 2 * width]
        return carry

    lax.fori_loop(0, chunks, again, 0)
    settle(lg.at[pl.ds(0, nc - 1), pl.ds(0, 1)], 0)
    for j in others:
        mine = lg.at[:, pl.ds(ab, 1)]
        remote(mine, mine, send.at[6], recv.at[6], peer_ab(j)).start()
    pair_rows = 2 * nc
    l8[0:nc] = lg[:, ab]
    l8[nc:pair_rows] = lg[:, ab]
    both = l8[...].reshape(pair_rows, lane)
    norm = 1.0 / math.sqrt(depth)
    odd = iota((pair_rows, lane), 0) // nc
    zlane = iota((pair_rows, lane), 1) // frames
    upper = []
    for s in range(2):
        mine = lax.rem(both, cells) if s == 0 else lax.div(both, cells)
        kz = lax.rem(mine, depth)
        r = lax.div(mine, depth)
        upper.append(r >= 2)
        here = lax.rem(r, 2) == odd
        for i in range(nab):
            zpos = (i * nc + ic) * slab + zlane
            angle = lax.rem(kz * zpos, depth).astype(F32) * (2.0 * math.pi / depth)
            pf[s, 0, i] = jnp.where(here, (jnp.cos(angle) * norm).astype(BF).astype(F32), 0.0)
            pf[s, 1, i] = jnp.where(here, (jnp.sin(angle) * -norm).astype(BF).astype(F32), 0.0)
    settle(vg.at[pl.ds(0, nf - 1)], 4)

    vt = [vg[:, p].reshape(frames, rank) for p in range(2)]
    rep = (iota((rank, 4 * rank), 0) == iota((rank, 4 * rank), 1) % rank).astype(F32).astype(BF)
    wide = [nn(vt[p], rep) for p in range(2)]
    block_of = iota((frames, 4 * rank), 1) // rank
    for blk in range(4):
        r_ = jnp.where(block_of == blk, wide[0], 0.0).astype(BF)
        i_ = jnp.where(block_of == blk, wide[1], 0.0).astype(BF)
        at = blk * frames
        vbt[at : at + frames, 0 : 4 * rank] = r_
        vbt[at : at + frames, 4 * rank : 8 * rank] = -i_
        at = (4 + blk) * frames
        vbt[at : at + frames, 0 : 4 * rank] = i_
        vbt[at : at + frames, 4 * rank : 8 * rank] = r_
    rep2 = (iota((sl, rank), 0) % rank == iota((sl, rank), 1)).astype(F32).astype(BF)
    same = iota((sl, lane), 0) // rank == iota((sl, lane), 1) // frames
    tall = [nt(rep2, jnp.concatenate([vt[p], vt[p]], 0)) for p in range(2)]
    r_ = jnp.where(same, tall[0], 0.0).astype(BF)
    i_ = jnp.where(same, tall[1], 0.0).astype(BF)
    vc[0:sl, 0:lane] = r_
    vc[0:sl, lane : 2 * lane] = i_
    vc[sl : 2 * sl, 0:lane] = -i_
    vc[sl : 2 * sl, lane : 2 * lane] = r_
    n_rows = GROUP * blocks
    out_row = iota((n_rows, n_rows), 0)
    in_row = iota((n_rows, n_rows), 1)
    spot = in_row // nc % GROUP * blocks + in_row % nc * nab + in_row // (nc * GROUP)
    permt[...] = (spot == out_row).astype(F32).astype(BF)
    settle(kg.at[pl.ds(0, nc - 1)], 5)
    kall = kg[...].reshape(nc * 16, 2 * lane)
    krow = iota((chunks * GROUP * nc, nc * 16), 0)
    kcol = iota((chunks * GROUP * nc, nc * 16), 1)
    pick = (krow % nc * 16 + krow // nc == kcol).astype(F32).astype(BF)
    kd[...] = nn(pick, kall).reshape(chunks, GROUP * nc, 2 * lane)
    lo8 = iota((pair_rows, lane), 1) < frames
    top = iota((pair_rows, lane), 0) < nc

    def parts_of(k, carry):
        settle(hr.at[k, pl.ds(0, nab - 1)], 1 + k)
        tiles = []
        for pair in range(GROUP // 2):
            at = pair * 2 * sl
            lhs = jnp.concatenate(
                [hr[k, :, p, :, at : at + 2 * sl].reshape(width, 2 * sl) for p in range(2)], 1
            )
            mixed = nt(lhs, vbt[...]).reshape(nab, ROWS * nc, 4 * lane)
            totals = []
            for c2 in range(2):
                re0, im0 = c2 * lane, (2 + c2) * lane
                got = []
                for s in range(2):
                    mr = jnp.where(
                        upper[s][None],
                        mixed[:, pair_rows:, re0 : re0 + lane],
                        mixed[:, :pair_rows, re0 : re0 + lane],
                    )
                    mi = jnp.where(
                        upper[s][None],
                        mixed[:, pair_rows:, im0 : im0 + lane],
                        mixed[:, :pair_rows, im0 : im0 + lane],
                    )
                    pr, pi = pf[s, 0], pf[s, 1]
                    got.append((jnp.sum(pr * mr - pi * mi, 0), jnp.sum(pr * mi + pi * mr, 0)))
                both_q = []
                for q in range(2):
                    keep = jnp.where(lo8, got[0][q], got[1][q])
                    fold = jnp.where(lo8, got[1][q], got[0][q])
                    total = keep + pltpu.roll(fold, frames, 1)
                    both_q.append(total + pltpu.roll(total, nc, 0))
                totals.append(both_q)
            tiles.append(
                jnp.concatenate([jnp.where(top, totals[0][q], totals[1][q]) for q in range(2)], 1)
            )
        zr[k, ic] = jnp.concatenate(tiles, 0).astype(BF)
        for j in range(1, nc):
            remote(
                zr.at[k, ic], zr.at[k, ic], send.at[7 + k], recv.at[7 + k], peer_c(j)
            ).start()
        return carry

    lax.fori_loop(0, chunks, parts_of, 0)
    settle(lg.at[:, pl.ds(0, nab - 1)], 6)
    lo = iota((blocks, lane), 1) < frames
    both = lg[...].reshape(blocks, lane)
    zpos = me * slab + iota((blocks, lane), 1) // frames
    for s in range(2):
        mine = lax.rem(both, cells) if s == 0 else lax.div(both, cells)
        kz = lax.rem(mine, depth)
        rowid[s] = lax.div(mine, depth)
        angle = lax.rem(kz * zpos, depth).astype(F32) * (2.0 * math.pi / depth)
        ph[s, 0] = (jnp.cos(angle) * norm).astype(BF).astype(F32)
        ph[s, 1] = (jnp.sin(angle) * -norm).astype(BF).astype(F32)
    for k in range(chunks):
        settle(zr.at[k, pl.ds(0, nc - 1)], 7 + k)
        total = zr[k, 0].astype(F32)
        for j in range(1, nc):
            total = total + zr[k, j].astype(F32)
        ra[k, ab] = (total - kd[k]).astype(BF)
        for j in others:
            remote(
                ra.at[k, ab], ra.at[k, ab], send.at[10 + k], recv.at[10 + k], peer_ab(j)
            ).start()
    gv[...] = jnp.zeros_like(gv)

    def spread(k, carry):
        settle(ra.at[k, pl.ds(0, nab - 1)], 10 + k)
        resid = nn(permt[...], ra[k].reshape(n_rows, 2 * lane))
        for c4 in range(GROUP):
            here = [
                resid[c4 * blocks : (c4 + 1) * blocks, q * lane : (q + 1) * lane] for q in range(2)
            ]
            flip = [pltpu.roll(x, frames, 1) for x in here]
            terms = []
            for s in range(2):
                xr_, xi_ = [
                    jnp.where(lo, a, b) if s == 0 else jnp.where(lo, b, a)
                    for a, b in zip(here, flip)
                ]
                pr, pi = ph[s, 0], ph[s, 1]
                terms.append((xr_ * pr + xi_ * pi, xi_ * pr - xr_ * pi))
            for r in range(ROWS):
                m0, m1 = rowid[0] == r, rowid[1] == r
                for q in range(2):
                    ea[k, c4, r * blocks : (r + 1) * blocks, q * lane : (q + 1) * lane] = (
                        jnp.where(m0, terms[0][q], 0.0) + jnp.where(m1, terms[1][q], 0.0)
                    ).astype(BF)
            gv[...] += nn(hn[k, c4], ea[k, c4])
        return carry

    lax.fori_loop(0, chunks, spread, 0)

    own = {}
    for p in range(2):
        for q in range(2):
            first = gv[p * sl : p * sl + rank, q * lane : (q + 1) * lane]
            second = gv[p * sl + rank : (p + 1) * sl, q * lane : (q + 1) * lane]
            own[p, q] = first + pltpu.roll(second, frames, 1)
    gre = (own[0, 0] + own[1, 1]) * scale
    gim = (own[0, 1] - own[1, 0]) * scale
    turned = jnp.transpose(jnp.concatenate([gre, gim, gre, gim], 0))
    half = span // 2
    first_half = iota((half, 4 * rank), 1) < 2 * rank
    for f in range(nf):
        gs[f] = jnp.where(
            first_half,
            turned[f * span : f * span + half],
            turned[f * span + half : (f + 1) * span],
        ).astype(BF)
    spot_cf = ic * nf + fr
    gz[spot_cf] = gs[fr]
    for j in range(1, nc * nf):
        remote(
            gs.at[lax.rem(fr + j % nf, nf)], gz.at[spot_cf], send.at[13], recv.at[13], peer_cf(j)
        ).start()

    def backward(k, carry):
        for c4 in range(GROUP):
            zc = nt(vc[...], ea[k, c4]).astype(BF)
            zg[k, c4 * sl : (c4 + 1) * sl, 0:width] = zc[0:sl]
            zg[k, c4 * sl : (c4 + 1) * sl, width : 2 * width] = zc[sl : 2 * sl]
        back = nn(zg[k], t2_ref[...])
        out = list(carry)
        for z in range(slab):
            re, im = out[2 * z], out[2 * z + 1]
            for c4 in range(GROUP):
                c = k * GROUP + c4
                mr, mi = mf[c, z : z + 1, :], mf[coils + c, z : z + 1, :]
                at = (c4 * slab + z) * rank
                br = back[at : at + rank, 0:width]
                bi = back[at : at + rank, width : 2 * width]
                re = re + mr * br + mi * bi
                im = im + mr * bi - mi * br
            out[2 * z], out[2 * z + 1] = re, im
        return tuple(out)

    zero = jnp.zeros((rank, width), F32)
    out = lax.fori_loop(0, chunks, backward, (zero,) * (2 * slab))
    for z in range(slab):
        for p in range(2):
            gout[p * rank : (p + 1) * rank, z] = out[2 * z + p].reshape(rank, 1, width)

    settle(gz.at[pl.ds(0, nc * nf - 1)], 13)
    gx[ab] = jnp.sum(gz[...].astype(F32), 0)
    for j in others:
        remote(gx.at[ab], gx.at[ab], send.at[14], recv.at[14], peer_ab(j)).start()
    settle(gx.at[pl.ds(0, nab - 1)], 14)
    total = jnp.sum(gx[...], 0)
    for q in range(2):
        for h in range(2):
            at = (2 * h + q) * rank
            fo[q, h * half : (h + 1) * half, :] = total[:, at : at + rank]


def finish(g_in, f_in, g_out, f_out, sems):
    copies = [
        pltpu.make_async_copy(g_in, g_out, sems.at[0]),
        pltpu.make_async_copy(f_in, f_out, sems.at[1]),
    ]
    for copy in copies:
        copy.start()
    for copy in copies:
        copy.wait()


SHAPES = {64: (4, 4, 4), 8: (2, 2, 2)}


def body(basis, coil_maps, factors, lines, kdata):
    n_cuts = lax.axis_size("cuts")
    nf = lax.axis_size("frame")
    na, nb, nc = SHAPES[n_cuts]
    rank, slab, width = basis.shape[1], basis.shape[2], basis.shape[4]
    coils = coil_maps.shape[1]
    chunks = coils // GROUP
    span = factors.shape[2]
    lpd = lines.shape[1]
    frames = span * nf
    lane = 2 * frames
    sl = slab * rank
    blocks = n_cuts
    n_rows = GROUP * blocks
    scale = 1.0 / math.sqrt(coils * lpd * n_cuts * basis.shape[3] * nf)
    table, table2 = (jnp.asarray(x, BF) for x in real_table(width, (na, nb, nc)))
    b = basis.transpose(0, 1, 3, 2, 4).reshape(2 * rank, slab, width)
    m = coil_maps.transpose(0, 1, 3, 2, 4).reshape(2 * coils, slab, width)
    v = factors.transpose(0, 2, 1)
    l = lines.T
    d = kdata.transpose(0, 3, 4, 2, 1).reshape(2 * coils, lpd, frames)
    dma = pltpu.SemaphoreType.DMA
    vm = pltpu.VMEM
    nab = na * nb
    scratch = [
        vm(b.shape, BF),
        vm(m.shape, BF),
        vm(l.shape, I32),
        vm(d.shape, BF),
        vm(table.shape, BF),
        vm(table.shape, BF),
        vm((slab, 2, rank, width), F32),
        vm(m.shape, F32),
        vm((1, lane), I32),
        vm((2 * nc, 1, lane), I32),
        vm((16, 2 * lane), F32),
        vm((chunks, GROUP * sl, 2 * width), BF),
        vm((chunks, nab, 2, ROWS * nc, GROUP * sl), BF),
        vm((chunks, nab, 2, ROWS * nc, GROUP * sl), BF),
        vm((chunks, GROUP, 2 * sl, width), BF),
        vm((8 * frames, 8 * rank), BF),
        vm((2 * sl, 2 * lane), BF),
        vm((2, 2, nab, 2 * nc, lane), F32),
        vm((2, 2, blocks, lane), F32),
        vm((2, blocks, lane), I32),
        vm((n_rows, n_rows), BF),
        vm((chunks, nc, GROUP * nc, 2 * lane), BF),
        vm((chunks, nab, GROUP * nc, 2 * lane), BF),
        vm((nc, nab, 1, lane), I32),
        vm((nf, 2, span, rank), BF),
        vm((nc, 16, 2 * lane), BF),
        vm((chunks, GROUP * nc, 2 * lane), F32),
        vm((chunks, GROUP, width, 2 * lane), BF),
        vm((chunks, GROUP * sl, 2 * width), BF),
        vm((2 * sl, 2 * lane), F32),
        vm((nf, span // 2, 4 * rank), BF),
        vm((nc * nf, span // 2, 4 * rank), BF),
        vm((nab, span // 2, 4 * rank), F32),
        dma((7,)),
        dma((15,)),
        dma((15,)),
    ]
    grad, fg = pl.pallas_call(
        functools.partial(kernel, (na, nb, nc, nf, chunks), scale),
        out_shape=(
            pltpu.VMEM((2 * rank, slab, 1, width), F32),
            pltpu.VMEM((2, span, rank), F32),
        ),
        in_specs=[pl.BlockSpec(memory_space=pl.ANY)] * 7,
        out_specs=[pl.BlockSpec(memory_space=pltpu.VMEM)] * 2,
        scratch_shapes=scratch,
        compiler_params=pltpu.CompilerParams(
            collective_id=0, has_side_effects=True, vmem_limit_bytes=24 * 1024 * 1024
        ),
    )(*[pltpu.with_memory_space_constraint(x, pltpu.HBM) for x in (b, m, v, l, d, table, table2)])
    grad, fg = pl.pallas_call(
        finish,
        out_shape=(
            jax.ShapeDtypeStruct(grad.shape, F32),
            jax.ShapeDtypeStruct(fg.shape, F32),
        ),
        in_specs=[pl.BlockSpec(memory_space=pl.ANY)] * 2,
        out_specs=[pl.BlockSpec(memory_space=pl.ANY)] * 2,
        scratch_shapes=[dma((2,))],
        compiler_params=pltpu.CompilerParams(vmem_limit_bytes=4 * 1024 * 1024),
    )(grad, fg)
    return grad.reshape(basis.shape), fg.transpose(0, 2, 1)


def solution(mesh):
    placed = (
        P(None, None, "cuts", "frame", None),
        P(None, None, "cuts", "frame", None),
        P(None, None, "frame"),
        P(None, "cuts"),
        P(None, None, "cuts", None, "frame"),
    )
    return jax.shard_map(
        body,
        mesh=mesh,
        in_specs=placed,
        out_specs=(P(None, None, "cuts", "frame", None), P(None, None, "frame")),
        check_vma=False,
    )
```

```python
import functools
import math

import jax
import jax.numpy as jnp
import numpy as np
from jax import lax
from jax.experimental import pallas as pl
from jax.experimental.pallas import tpu as pltpu
from jax.sharding import PartitionSpec as P

BF = jnp.bfloat16
F32 = jnp.float32
I32 = jnp.int32
GROUP = 4
ROWS = 4


def real_table(size, shape):
    index = np.arange(size)
    angle = (index[:, None] * index[None, :] % size) * (2.0 * math.pi / size)
    cosine, sine = np.cos(angle) / math.sqrt(size), np.sin(angle) / math.sqrt(size)
    whole = np.stack([np.concatenate([cosine, sine], 1), np.concatenate([-sine, cosine], 1)])
    whole = whole.reshape((2,) + tuple(shape) + (ROWS, 2 * size))
    first = whole.transpose(1, 2, 0, 4, 3, 5).reshape(2 * size, 2 * size)
    second = whole.transpose(0, 4, 3, 1, 2, 5).reshape(2 * size, 2 * size)
    return first, second


def nn(a, b):
    return jnp.dot(a, b, preferred_element_type=F32)


def nt(a, b):
    return lax.dot_general(a, b, (((1,), (1,)), ((), ())), preferred_element_type=F32)


def iota(shape, axis):
    return lax.broadcasted_iota(I32, shape, axis)


def kernel(
    dims,
    scale,
    b_hbm,
    m_hbm,
    v_hbm,
    l_hbm,
    d_hbm,
    t_hbm,
    t2_hbm,
    gout,
    fo,
    bv,
    mv,
    lv,
    dv,
    t_ref,
    t2_ref,
    bf,
    mf,
    lt,
    l8,
    kt,
    img,
    ht,
    hr,
    vbt,
    vc,
    pf,
    ph,
    rowid,
    permt,
    zr,
    ra,
    lg,
    vg,
    kg,
    kd,
    ea,
    zg,
    gv,
    hrt,
    ef,
    gs,
    gz,
    gx,
    local,
    send,
    recv,
):
    na, nb, nc, nf, chunks = dims
    coils = chunks * GROUP
    rank = b_hbm.shape[0] // 2
    slab, width = b_hbm.shape[1:]
    span = v_hbm.shape[1]
    frames = span * nf
    nab = na * nb
    blocks = nab * nc
    depth = slab * blocks
    cells = depth * ROWS
    me = lax.axis_index("cuts")
    fr = lax.axis_index("frame")
    ia, ib, ic = me // (nb * nc), (me // nc) % nb, me % nc
    ab = ia * nb + ib
    lane = 2 * frames
    sl = slab * rank
    mesh_id = pl.DeviceIdType.MESH

    def cut(a, b, c):
        return a * (nb * nc) + b * nc + c

    def peer_c(j):
        return {"cuts": cut(ia, ib, lax.rem(ic + j, nc))}

    def peer_f(j):
        return {"frame": lax.rem(fr + j, nf)}

    def peer_ab(j):
        return {"cuts": cut(lax.rem(ia + j // nb, na), lax.rem(ib + j % nb, nb), ic)}

    def peer_cf(j):
        return {
            "cuts": cut(ia, ib, lax.rem(ic + j // nf, nc)),
            "frame": lax.rem(fr + j % nf, nf),
        }

    def remote(src, dst, s, r, who):
        return pltpu.make_async_remote_copy(
            src_ref=src, dst_ref=dst, send_sem=s, recv_sem=r, device_id=who, device_id_type=mesh_id
        )

    def far(j):
        da, db = j // nb, j % nb
        da, db = min(da, na - da), min(db, nb - db)
        return (-da, -db, j)

    others = sorted(range(1, nab), key=far)
    everyone = [peer_ab(j) for j in others] + [peer_cf(j) for j in range(1, nc * nf)]
    barrier = pltpu.get_barrier_semaphore()
    for who in everyone:
        pl.semaphore_signal(barrier, inc=1, device_id=who, device_id_type=mesh_id)

    def settle(block, at):
        pltpu.make_async_copy(block, block, send.at[at]).wait()
        pltpu.make_async_copy(block, block, recv.at[at]).wait()

    loads = [
        pltpu.make_async_copy(l_hbm, lv, local.at[0]),
        pltpu.make_async_copy(b_hbm, bv, local.at[1]),
        pltpu.make_async_copy(m_hbm, mv, local.at[2]),
        pltpu.make_async_copy(t_hbm, t_ref, local.at[3]),
        pltpu.make_async_copy(v_hbm, vg.at[fr], local.at[4]),
        pltpu.make_async_copy(d_hbm, dv, local.at[5]),
        pltpu.make_async_copy(t2_hbm, t2_ref, local.at[6]),
    ]
    for copy in loads:
        copy.start()
    loads[0].wait()
    row = lv[0:1, :] + lv[1:2, :] * cells
    lt[0:1, 0:frames] = row
    lt[0:1, frames:lane] = row
    lg[ic, pl.ds(ab, 1)] = lt[...][None]
    loads[1].wait()
    loads[2].wait()
    for p in range(2):
        x = bv[p * rank : (p + 1) * rank].astype(F32)
        for z in range(slab):
            bf[z, p] = x[:, z, :]
    mf[...] = mv[...].astype(F32)
    loads[3].wait()
    loads[4].wait()

    def forward(k, carry):
        for c4 in range(GROUP):
            c = k * GROUP + c4
            for z in range(slab):
                mr, mi = mf[c, z : z + 1, :], mf[coils + c, z : z + 1, :]
                br, bi = bf[z, 0], bf[z, 1]
                at = (c4 * slab + z) * rank
                img[k, at : at + rank, 0:width] = (mr * br - mi * bi).astype(BF)
                img[k, at : at + rank, width : 2 * width] = (mr * bi + mi * br).astype(BF)
        ht[k] = nt(t_ref[...], img[k]).astype(BF).reshape(nab, 2, ROWS * nc, GROUP * sl)
        hr[k, ab] = ht[k, ab]
        return carry

    lax.fori_loop(0, chunks, forward, 0)

    pl.semaphore_wait(barrier, len(everyone))

    for j in range(1, nc):
        own_line = lg.at[ic, pl.ds(ab, 1)]
        remote(own_line, own_line, send.at[0], recv.at[0], peer_c(j)).start()
    for k in range(chunks):
        for j in others:
            to = lax.rem(ia + j // nb, na) * nb + lax.rem(ib + j % nb, nb)
            remote(
                ht.at[k, to], hr.at[k, ab], send.at[1 + k], recv.at[1 + k], peer_ab(j)
            ).start()
    for j in range(1, nf):
        remote(vg.at[fr], vg.at[fr], send.at[4], recv.at[4], peer_f(j)).start()
    loads[5].wait()
    kt[...] = jnp.zeros_like(kt)
    for q in range(2):
        x = dv[q * coils : (q + 1) * coils].astype(F32)
        for s in range(2):
            kt[0:coils, q * lane + s * frames : q * lane + (s + 1) * frames] = x[:, s, :]
    kg[ic] = kt[...].astype(BF)
    for j in range(1, nc):
        remote(kg.at[ic], kg.at[ic], send.at[5], recv.at[5], peer_c(j)).start()
    loads[6].wait()
    settle(lg.at[pl.ds(0, nc - 1), pl.ds(0, 1)], 0)
    for j in others:
        mine = lg.at[:, pl.ds(ab, 1)]
        remote(mine, mine, send.at[6], recv.at[6], peer_ab(j)).start()
    pair_rows = 2 * nc
    l8[0:nc] = lg[:, ab]
    l8[nc:pair_rows] = lg[:, ab]
    both = l8[...].reshape(pair_rows, lane)
    norm = 1.0 / math.sqrt(depth)
    odd = iota((pair_rows, lane), 0) // nc
    zlane = iota((pair_rows, lane), 1) // frames
    upper = []
    for s in range(2):
        mine = lax.rem(both, cells) if s == 0 else lax.div(both, cells)
        kz = lax.rem(mine, depth)
        r = lax.div(mine, depth)
        upper.append(r >= 2)
        here = lax.rem(r, 2) == odd
        for i in range(nab):
            zpos = (i * nc + ic) * slab + zlane
            angle = lax.rem(kz * zpos, depth).astype(F32) * (2.0 * math.pi / depth)
            pf[s, 0, i] = jnp.where(here, (jnp.cos(angle) * norm).astype(BF).astype(F32), 0.0)
            pf[s, 1, i] = jnp.where(here, (jnp.sin(angle) * -norm).astype(BF).astype(F32), 0.0)
    settle(vg.at[pl.ds(0, nf - 1)], 4)

    vt = [vg[:, p].reshape(frames, rank) for p in range(2)]
    rep = (iota((rank, 4 * rank), 0) == iota((rank, 4 * rank), 1) % rank).astype(F32).astype(BF)
    wide = [nn(vt[p], rep) for p in range(2)]
    block_of = iota((frames, 4 * rank), 1) // rank
    for blk in range(4):
        r_ = jnp.where(block_of == blk, wide[0], 0.0).astype(BF)
        i_ = jnp.where(block_of == blk, wide[1], 0.0).astype(BF)
        at = blk * frames
        vbt[at : at + frames, 0 : 4 * rank] = r_
        vbt[at : at + frames, 4 * rank : 8 * rank] = -i_
        at = (4 + blk) * frames
        vbt[at : at + frames, 0 : 4 * rank] = i_
        vbt[at : at + frames, 4 * rank : 8 * rank] = r_
    rep2 = (iota((sl, rank), 0) % rank == iota((sl, rank), 1)).astype(F32).astype(BF)
    same = iota((sl, lane), 0) // rank == iota((sl, lane), 1) // frames
    tall = [nt(rep2, jnp.concatenate([vt[p], vt[p]], 0)) for p in range(2)]
    r_ = jnp.where(same, tall[0], 0.0).astype(BF)
    i_ = jnp.where(same, tall[1], 0.0).astype(BF)
    vc[0:sl, 0:lane] = r_
    vc[0:sl, lane : 2 * lane] = i_
    vc[sl : 2 * sl, 0:lane] = -i_
    vc[sl : 2 * sl, lane : 2 * lane] = r_
    n_rows = GROUP * blocks
    out_row = iota((n_rows, n_rows), 0)
    in_row = iota((n_rows, n_rows), 1)
    spot = in_row // nc % GROUP * blocks + in_row % nc * nab + in_row // (nc * GROUP)
    permt[...] = (spot == out_row).astype(F32).astype(BF)
    settle(kg.at[pl.ds(0, nc - 1)], 5)
    kall = kg[...].reshape(nc * 16, 2 * lane)
    krow = iota((chunks * GROUP * nc, nc * 16), 0)
    kcol = iota((chunks * GROUP * nc, nc * 16), 1)
    pick = (krow % nc * 16 + krow // nc == kcol).astype(F32).astype(BF)
    kd[...] = nn(pick, kall).reshape(chunks, GROUP * nc, 2 * lane)
    lo8 = iota((pair_rows, lane), 1) < frames
    top = iota((pair_rows, lane), 0) < nc

    def hybrids(k, pair):
        at = pair * 2 * sl
        return jnp.concatenate(
            [hr[k, :, p, :, at : at + 2 * sl].reshape(width, 2 * sl) for p in range(2)], 1
        )

    def residual(k):
        settle(zr.at[k, pl.ds(0, nc - 1)], 7 + k)
        total = zr[k, 0].astype(F32)
        for j in range(1, nc):
            total = total + zr[k, j].astype(F32)
        ra[k, ab] = (total - kd[k]).astype(BF)

    def gather(k):
        for j in others:
            remote(
                ra.at[k, ab], ra.at[k, ab], send.at[10 + k], recv.at[10 + k], peer_ab(j)
            ).start()

    def factor_part(k):
        whole = ra[k, ab].astype(F32)
        for c4 in range(GROUP):
            at = c4 // 2 * pair_rows
            here = []
            for q in range(2):
                tile = whole[at : at + pair_rows, q * lane : (q + 1) * lane]
                other = pltpu.roll(tile, nc, 0)
                here.append(
                    jnp.where(top, tile, other) if c4 % 2 == 0 else jnp.where(top, other, tile)
                )
            flip = [pltpu.roll(x, frames, 1) for x in here]
            values = []
            for s in range(2):
                for a, b in zip(here, flip):
                    x = jnp.where(lo8, a, b) if s == 0 else jnp.where(lo8, b, a)
                    values.append((jnp.where(upper[s], 0.0, x), jnp.where(upper[s], x, 0.0)))
            for i in range(nab):
                p0, i0, p1, i1 = pf[0, 0, i], pf[0, 1, i], pf[1, 0, i], pf[1, 1, i]
                re, im = [], []
                for h in range(2):
                    x0, y0, x1, y1 = [v[h] for v in values]
                    re.append((p0 * x0 + i0 * y0) + (p1 * x1 + i1 * y1))
                    im.append((p0 * y0 - i0 * x0) + (p1 * y1 - i1 * x1))
                row = c4 * width + i * 2 * pair_rows
                ef[row : row + 2 * pair_rows, 0:lane] = jnp.concatenate(re, 0).astype(BF)
                ef[row : row + 2 * pair_rows, lane : 2 * lane] = jnp.concatenate(im, 0).astype(BF)
        gv[...] += nn(hrt[k], ef[...])

    def turn(k):
        for p in range(2):
            t = jnp.transpose(hr[k, :, p].reshape(width, GROUP * sl))
            for c4 in range(GROUP):
                hrt[k, p * sl : (p + 1) * sl, c4 * width : (c4 + 1) * width] = t[
                    c4 * sl : (c4 + 1) * sl
                ]

    gv[...] = jnp.zeros_like(gv)

    def parts_of(k, carry):
        settle(hr.at[k, pl.ds(0, nab - 1)], 1 + k)
        tiles = []
        for pair in range(GROUP // 2):
            mixed = nt(hybrids(k, pair), vbt[...]).reshape(nab, ROWS * nc, 4 * lane)
            totals = []
            for c2 in range(2):
                re0, im0 = c2 * lane, (2 + c2) * lane
                got = []
                for s in range(2):
                    mr = jnp.where(
                        upper[s][None],
                        mixed[:, pair_rows:, re0 : re0 + lane],
                        mixed[:, :pair_rows, re0 : re0 + lane],
                    )
                    mi = jnp.where(
                        upper[s][None],
                        mixed[:, pair_rows:, im0 : im0 + lane],
                        mixed[:, :pair_rows, im0 : im0 + lane],
                    )
                    pr, pi = pf[s, 0], pf[s, 1]
                    got.append((jnp.sum(pr * mr - pi * mi, 0), jnp.sum(pr * mi + pi * mr, 0)))
                both_q = []
                for q in range(2):
                    keep = jnp.where(lo8, got[0][q], got[1][q])
                    fold = jnp.where(lo8, got[1][q], got[0][q])
                    total = keep + pltpu.roll(fold, frames, 1)
                    both_q.append(total + pltpu.roll(total, nc, 0))
                totals.append(both_q)
            tiles.append(
                jnp.concatenate([jnp.where(top, totals[0][q], totals[1][q]) for q in range(2)], 1)
            )
        zr[k, ic] = jnp.concatenate(tiles, 0).astype(BF)
        for j in range(1, nc):
            remote(
                zr.at[k, ic], zr.at[k, ic], send.at[7 + k], recv.at[7 + k], peer_c(j)
            ).start()
        turn(k)

        @pl.when(k >= 1)
        def _():
            residual(k - 1)
            factor_part(k - 1)

        return carry

    lax.fori_loop(0, chunks, parts_of, 0)
    for k in range(chunks - 1):
        gather(k)
    settle(lg.at[:, pl.ds(0, nab - 1)], 6)
    lo = iota((blocks, lane), 1) < frames
    both = lg[...].reshape(blocks, lane)
    zpos = me * slab + iota((blocks, lane), 1) // frames
    for s in range(2):
        mine = lax.rem(both, cells) if s == 0 else lax.div(both, cells)
        kz = lax.rem(mine, depth)
        rowid[s] = lax.div(mine, depth)
        angle = lax.rem(kz * zpos, depth).astype(F32) * (2.0 * math.pi / depth)
        ph[s, 0] = (jnp.cos(angle) * norm).astype(BF).astype(F32)
        ph[s, 1] = (jnp.sin(angle) * -norm).astype(BF).astype(F32)
    residual(chunks - 1)
    gather(chunks - 1)
    factor_part(chunks - 1)

    own = {}
    for p in range(2):
        for q in range(2):
            first = gv[p * sl : p * sl + rank, q * lane : (q + 1) * lane]
            second = gv[p * sl + rank : (p + 1) * sl, q * lane : (q + 1) * lane]
            own[p, q] = first + pltpu.roll(second, frames, 1)
    gre = (own[0, 0] + own[1, 1]) * scale
    gim = (own[0, 1] - own[1, 0]) * scale
    turned = jnp.transpose(jnp.concatenate([gre, gim, gre, gim], 0))
    half = span // 2
    first_half = iota((half, 4 * rank), 1) < 2 * rank
    for f in range(nf):
        gs[f] = jnp.where(
            first_half,
            turned[f * span : f * span + half],
            turned[f * span + half : (f + 1) * span],
        ).astype(BF)
    spot_cf = ic * nf + fr
    gz[spot_cf] = gs[fr]
    for j in range(1, nc * nf):
        remote(
            gs.at[lax.rem(fr + j % nf, nf)], gz.at[spot_cf], send.at[13], recv.at[13], peer_cf(j)
        ).start()
    def spread(k, carry):
        settle(ra.at[k, pl.ds(0, nab - 1)], 10 + k)
        resid = nn(permt[...], ra[k].reshape(n_rows, 2 * lane))
        for c4 in range(GROUP):
            here = [
                resid[c4 * blocks : (c4 + 1) * blocks, q * lane : (q + 1) * lane] for q in range(2)
            ]
            flip = [pltpu.roll(x, frames, 1) for x in here]
            terms = []
            for s in range(2):
                xr_, xi_ = [
                    jnp.where(lo, a, b) if s == 0 else jnp.where(lo, b, a)
                    for a, b in zip(here, flip)
                ]
                pr, pi = ph[s, 0], ph[s, 1]
                terms.append((xr_ * pr + xi_ * pi, xi_ * pr - xr_ * pi))
            for r in range(ROWS):
                m0, m1 = rowid[0] == r, rowid[1] == r
                for q in range(2):
                    ea[k, c4, r * blocks : (r + 1) * blocks, q * lane : (q + 1) * lane] = (
                        jnp.where(m0, terms[0][q], 0.0) + jnp.where(m1, terms[1][q], 0.0)
                    ).astype(BF)
        return carry

    lax.fori_loop(0, chunks, spread, 0)

    settle(gz.at[pl.ds(0, nc * nf - 1)], 13)
    gx[ab] = jnp.sum(gz[...].astype(F32), 0)
    for j in others:
        remote(gx.at[ab], gx.at[ab], send.at[14], recv.at[14], peer_ab(j)).start()

    def backward(k, carry):
        for c4 in range(GROUP):
            zc = nt(vc[...], ea[k, c4]).astype(BF)
            zg[k, c4 * sl : (c4 + 1) * sl, 0:width] = zc[0:sl]
            zg[k, c4 * sl : (c4 + 1) * sl, width : 2 * width] = zc[sl : 2 * sl]
        back = nn(zg[k], t2_ref[...])
        out = list(carry)
        for z in range(slab):
            re, im = out[2 * z], out[2 * z + 1]
            for c4 in range(GROUP):
                c = k * GROUP + c4
                mr, mi = mf[c, z : z + 1, :], mf[coils + c, z : z + 1, :]
                at = (c4 * slab + z) * rank
                br = back[at : at + rank, 0:width]
                bi = back[at : at + rank, width : 2 * width]
                re = re + mr * br + mi * bi
                im = im + mr * bi - mi * br
            out[2 * z], out[2 * z + 1] = re, im
        return tuple(out)

    zero = jnp.zeros((rank, width), F32)
    out = lax.fori_loop(0, chunks, backward, (zero,) * (2 * slab))
    for z in range(slab):
        for p in range(2):
            gout[p * rank : (p + 1) * rank, z] = out[2 * z + p].reshape(rank, 1, width)
    settle(gx.at[pl.ds(0, nab - 1)], 14)
    total = jnp.sum(gx[...], 0)
    for q in range(2):
        for h in range(2):
            at = (2 * h + q) * rank
            fo[q, h * half : (h + 1) * half, :] = total[:, at : at + rank]


def finish(g_in, f_in, g_out, f_out, sems):
    copies = [
        pltpu.make_async_copy(g_in, g_out, sems.at[0]),
        pltpu.make_async_copy(f_in, f_out, sems.at[1]),
    ]
    for copy in copies:
        copy.start()
    for copy in copies:
        copy.wait()


SHAPES = {64: (4, 4, 4), 8: (2, 2, 2)}


def body(basis, coil_maps, factors, lines, kdata):
    n_cuts = lax.axis_size("cuts")
    nf = lax.axis_size("frame")
    na, nb, nc = SHAPES[n_cuts]
    rank, slab, width = basis.shape[1], basis.shape[2], basis.shape[4]
    coils = coil_maps.shape[1]
    chunks = coils // GROUP
    span = factors.shape[2]
    lpd = lines.shape[1]
    frames = span * nf
    lane = 2 * frames
    sl = slab * rank
    blocks = n_cuts
    n_rows = GROUP * blocks
    scale = 1.0 / math.sqrt(coils * lpd * n_cuts * basis.shape[3] * nf)
    table, table2 = (jnp.asarray(x, BF) for x in real_table(width, (na, nb, nc)))
    b = basis.transpose(0, 1, 3, 2, 4).reshape(2 * rank, slab, width)
    m = coil_maps.transpose(0, 1, 3, 2, 4).reshape(2 * coils, slab, width)
    v = factors.transpose(0, 2, 1)
    l = lines.T
    d = kdata.transpose(0, 3, 4, 2, 1).reshape(2 * coils, lpd, frames)
    dma = pltpu.SemaphoreType.DMA
    vm = pltpu.VMEM
    nab = na * nb
    scratch = [
        vm(b.shape, BF),
        vm(m.shape, BF),
        vm(l.shape, I32),
        vm(d.shape, BF),
        vm(table.shape, BF),
        vm(table.shape, BF),
        vm((slab, 2, rank, width), F32),
        vm(m.shape, F32),
        vm((1, lane), I32),
        vm((2 * nc, 1, lane), I32),
        vm((16, 2 * lane), F32),
        vm((chunks, GROUP * sl, 2 * width), BF),
        vm((chunks, nab, 2, ROWS * nc, GROUP * sl), BF),
        vm((chunks, nab, 2, ROWS * nc, GROUP * sl), BF),
        vm((8 * frames, 8 * rank), BF),
        vm((2 * sl, 2 * lane), BF),
        vm((2, 2, nab, 2 * nc, lane), F32),
        vm((2, 2, blocks, lane), F32),
        vm((2, blocks, lane), I32),
        vm((n_rows, n_rows), BF),
        vm((chunks, nc, GROUP * nc, 2 * lane), BF),
        vm((chunks, nab, GROUP * nc, 2 * lane), BF),
        vm((nc, nab, 1, lane), I32),
        vm((nf, 2, span, rank), BF),
        vm((nc, 16, 2 * lane), BF),
        vm((chunks, GROUP * nc, 2 * lane), F32),
        vm((chunks, GROUP, width, 2 * lane), BF),
        vm((chunks, GROUP * sl, 2 * width), BF),
        vm((2 * sl, 2 * lane), F32),
        vm((chunks, 2 * sl, GROUP * width), BF),
        vm((GROUP * width, 2 * lane), BF),
        vm((nf, span // 2, 4 * rank), BF),
        vm((nc * nf, span // 2, 4 * rank), BF),
        vm((nab, span // 2, 4 * rank), F32),
        dma((7,)),
        dma((15,)),
        dma((15,)),
    ]
    grad, fg = pl.pallas_call(
        functools.partial(kernel, (na, nb, nc, nf, chunks), scale),
        out_shape=(
            pltpu.VMEM((2 * rank, slab, 1, width), F32),
            pltpu.VMEM((2, span, rank), F32),
        ),
        in_specs=[pl.BlockSpec(memory_space=pl.ANY)] * 7,
        out_specs=[pl.BlockSpec(memory_space=pltpu.VMEM)] * 2,
        scratch_shapes=scratch,
        compiler_params=pltpu.CompilerParams(
            collective_id=0, has_side_effects=True, vmem_limit_bytes=24 * 1024 * 1024
        ),
    )(*[pltpu.with_memory_space_constraint(x, pltpu.HBM) for x in (b, m, v, l, d, table, table2)])
    grad, fg = pl.pallas_call(
        finish,
        out_shape=(
            jax.ShapeDtypeStruct(grad.shape, F32),
            jax.ShapeDtypeStruct(fg.shape, F32),
        ),
        in_specs=[pl.BlockSpec(memory_space=pl.ANY)] * 2,
        out_specs=[pl.BlockSpec(memory_space=pl.ANY)] * 2,
        scratch_shapes=[dma((2,))],
        compiler_params=pltpu.CompilerParams(vmem_limit_bytes=4 * 1024 * 1024),
    )(grad, fg)
    return grad.reshape(basis.shape), fg.transpose(0, 2, 1)


def solution(mesh):
    placed = (
        P(None, None, "cuts", "frame", None),
        P(None, None, "cuts", "frame", None),
        P(None, None, "frame"),
        P(None, "cuts"),
        P(None, None, "cuts", None, "frame"),
    )
    return jax.shard_map(
        body,
        mesh=mesh,
        in_specs=placed,
        out_specs=(P(None, None, "cuts", "frame", None), P(None, None, "frame")),
        check_vma=False,
    )
```

```python
import functools
import math

import jax
import jax.numpy as jnp
import numpy as np
from jax import lax
from jax.experimental import pallas as pl
from jax.experimental.pallas import tpu as pltpu
from jax.sharding import PartitionSpec as P

BF = jnp.bfloat16
F32 = jnp.float32
I32 = jnp.int32
GROUP = 4
ROWS = 4


def real_table(size, shape):
    index = np.arange(size)
    angle = (index[:, None] * index[None, :] % size) * (2.0 * math.pi / size)
    cosine, sine = np.cos(angle) / math.sqrt(size), np.sin(angle) / math.sqrt(size)
    whole = np.stack([np.concatenate([cosine, sine], 1), np.concatenate([-sine, cosine], 1)])
    whole = whole.reshape((2,) + tuple(shape) + (ROWS, 2 * size))
    first = whole.transpose(1, 2, 0, 4, 3, 5).reshape(2 * size, 2 * size)
    second = whole.transpose(0, 4, 3, 1, 2, 5).reshape(2 * size, 2 * size)
    return first, second


def nn(a, b):
    return jnp.dot(a, b, preferred_element_type=F32)


def nt(a, b):
    return lax.dot_general(a, b, (((1,), (1,)), ((), ())), preferred_element_type=F32)


def iota(shape, axis):
    return lax.broadcasted_iota(I32, shape, axis)


def kernel(
    dims,
    scale,
    b_hbm,
    m_hbm,
    v_hbm,
    l_hbm,
    d_hbm,
    t_hbm,
    t2_hbm,
    gout,
    fo,
    bv,
    mv,
    lv,
    dv,
    t_ref,
    t2_ref,
    bf,
    mf,
    lt,
    l8,
    kt,
    img,
    ht,
    hr,
    vbt,
    vc,
    pf,
    ph,
    rowid,
    permt,
    zr,
    ra,
    lg,
    vg,
    kg,
    kd,
    ea,
    zg,
    gv,
    hrt,
    ef,
    mx,
    gs,
    gz,
    gx,
    local,
    send,
    recv,
):
    na, nb, nc, nf, chunks = dims
    coils = chunks * GROUP
    rank = b_hbm.shape[0] // 2
    slab, width = b_hbm.shape[1:]
    span = v_hbm.shape[1]
    frames = span * nf
    nab = na * nb
    blocks = nab * nc
    depth = slab * blocks
    cells = depth * ROWS
    me = lax.axis_index("cuts")
    fr = lax.axis_index("frame")
    ia, ib, ic = me // (nb * nc), (me // nc) % nb, me % nc
    ab = ia * nb + ib
    lane = 2 * frames
    sl = slab * rank
    mesh_id = pl.DeviceIdType.MESH

    def cut(a, b, c):
        return a * (nb * nc) + b * nc + c

    def peer_c(j):
        return {"cuts": cut(ia, ib, lax.rem(ic + j, nc))}

    def peer_f(j):
        return {"frame": lax.rem(fr + j, nf)}

    def peer_ab(j):
        return {"cuts": cut(lax.rem(ia + j // nb, na), lax.rem(ib + j % nb, nb), ic)}

    def peer_cf(j):
        return {
            "cuts": cut(ia, ib, lax.rem(ic + j // nf, nc)),
            "frame": lax.rem(fr + j % nf, nf),
        }

    def remote(src, dst, s, r, who):
        return pltpu.make_async_remote_copy(
            src_ref=src, dst_ref=dst, send_sem=s, recv_sem=r, device_id=who, device_id_type=mesh_id
        )

    def far(j):
        da, db = j // nb, j % nb
        da, db = min(da, na - da), min(db, nb - db)
        return (-da, -db, j)

    others = sorted(range(1, nab), key=far)
    everyone = [peer_ab(j) for j in others] + [peer_cf(j) for j in range(1, nc * nf)]
    barrier = pltpu.get_barrier_semaphore()
    for who in everyone:
        pl.semaphore_signal(barrier, inc=1, device_id=who, device_id_type=mesh_id)

    def settle(block, at):
        pltpu.make_async_copy(block, block, send.at[at]).wait()
        pltpu.make_async_copy(block, block, recv.at[at]).wait()

    loads = [
        pltpu.make_async_copy(l_hbm, lv, local.at[0]),
        pltpu.make_async_copy(b_hbm, bv, local.at[1]),
        pltpu.make_async_copy(m_hbm, mv, local.at[2]),
        pltpu.make_async_copy(t_hbm, t_ref, local.at[3]),
        pltpu.make_async_copy(v_hbm, vg.at[fr], local.at[4]),
        pltpu.make_async_copy(d_hbm, dv, local.at[5]),
        pltpu.make_async_copy(t2_hbm, t2_ref, local.at[6]),
    ]
    for copy in loads:
        copy.start()
    loads[0].wait()
    row = lv[0:1, :] + lv[1:2, :] * cells
    lt[0:1, 0:frames] = row
    lt[0:1, frames:lane] = row
    lg[ic, pl.ds(ab, 1)] = lt[...][None]
    loads[1].wait()
    loads[2].wait()
    for p in range(2):
        x = bv[p * rank : (p + 1) * rank].astype(F32)
        for z in range(slab):
            bf[z, p] = x[:, z, :]
    mf[...] = mv[...].astype(F32)
    loads[3].wait()
    loads[4].wait()

    def forward(k, carry):
        for c4 in range(GROUP):
            c = k * GROUP + c4
            for z in range(slab):
                mr, mi = mf[c, z : z + 1, :], mf[coils + c, z : z + 1, :]
                br, bi = bf[z, 0], bf[z, 1]
                at = (c4 * slab + z) * rank
                img[k, at : at + rank, 0:width] = (mr * br - mi * bi).astype(BF)
                img[k, at : at + rank, width : 2 * width] = (mr * bi + mi * br).astype(BF)
        ht[k] = nt(t_ref[...], img[k]).astype(BF).reshape(nab, 2, ROWS * nc, GROUP * sl)
        hr[k, ab] = ht[k, ab]
        return carry

    lax.fori_loop(0, chunks, forward, 0)

    pl.semaphore_wait(barrier, len(everyone))

    for j in range(1, nc):
        own_line = lg.at[ic, pl.ds(ab, 1)]
        remote(own_line, own_line, send.at[0], recv.at[0], peer_c(j)).start()
    def exchange(k):
        for j in others:
            to = lax.rem(ia + j // nb, na) * nb + lax.rem(ib + j % nb, nb)
            remote(
                ht.at[k, to], hr.at[k, ab], send.at[1 + k], recv.at[1 + k], peer_ab(j)
            ).start()

    exchange(0)

    @pl.when(lax.rem(fr, 2) == 0)
    def _():
        for k in range(1, chunks):
            exchange(k)

    for j in range(1, nf):
        remote(vg.at[fr], vg.at[fr], send.at[4], recv.at[4], peer_f(j)).start()
    loads[5].wait()
    kt[...] = jnp.zeros_like(kt)
    for q in range(2):
        x = dv[q * coils : (q + 1) * coils].astype(F32)
        for s in range(2):
            kt[0:coils, q * lane + s * frames : q * lane + (s + 1) * frames] = x[:, s, :]
    kg[ic] = kt[...].astype(BF)
    for j in range(1, nc):
        remote(kg.at[ic], kg.at[ic], send.at[5], recv.at[5], peer_c(j)).start()
    loads[6].wait()
    settle(lg.at[pl.ds(0, nc - 1), pl.ds(0, 1)], 0)
    for j in others:
        mine = lg.at[:, pl.ds(ab, 1)]
        remote(mine, mine, send.at[6], recv.at[6], peer_ab(j)).start()

    @pl.when(lax.rem(fr, 2) == 1)
    def _():
        for k in range(1, chunks):
            exchange(k)

    pair_rows = 2 * nc
    l8[0:nc] = lg[:, ab]
    l8[nc:pair_rows] = lg[:, ab]
    both = l8[...].reshape(pair_rows, lane)
    norm = 1.0 / math.sqrt(depth)
    odd = iota((pair_rows, lane), 0) // nc
    zlane = iota((pair_rows, lane), 1) // frames
    upper = []
    for s in range(2):
        mine = lax.rem(both, cells) if s == 0 else lax.div(both, cells)
        kz = lax.rem(mine, depth)
        r = lax.div(mine, depth)
        upper.append(r >= 2)
        here = lax.rem(r, 2) == odd
        for i in range(nab):
            zpos = (i * nc + ic) * slab + zlane
            angle = lax.rem(kz * zpos, depth).astype(F32) * (2.0 * math.pi / depth)
            pf[s, 0, i] = jnp.where(here, (jnp.cos(angle) * norm).astype(BF).astype(F32), 0.0)
            pf[s, 1, i] = jnp.where(here, (jnp.sin(angle) * -norm).astype(BF).astype(F32), 0.0)
    settle(vg.at[pl.ds(0, nf - 1)], 4)

    vt = [vg[:, p].reshape(frames, rank) for p in range(2)]
    rep = (iota((rank, 4 * rank), 0) == iota((rank, 4 * rank), 1) % rank).astype(F32).astype(BF)
    wide = [nn(vt[p], rep) for p in range(2)]
    block_of = iota((frames, 4 * rank), 1) // rank
    for blk in range(4):
        r_ = jnp.where(block_of == blk, wide[0], 0.0).astype(BF)
        i_ = jnp.where(block_of == blk, wide[1], 0.0).astype(BF)
        at = blk * frames
        vbt[at : at + frames, 0 : 4 * rank] = r_
        vbt[at : at + frames, 4 * rank : 8 * rank] = -i_
        at = (4 + blk) * frames
        vbt[at : at + frames, 0 : 4 * rank] = i_
        vbt[at : at + frames, 4 * rank : 8 * rank] = r_
    rep2 = (iota((sl, rank), 0) % rank == iota((sl, rank), 1)).astype(F32).astype(BF)
    same = iota((sl, lane), 0) // rank == iota((sl, lane), 1) // frames
    tall = [nt(rep2, jnp.concatenate([vt[p], vt[p]], 0)) for p in range(2)]
    r_ = jnp.where(same, tall[0], 0.0).astype(BF)
    i_ = jnp.where(same, tall[1], 0.0).astype(BF)
    vc[0:sl, 0:lane] = r_
    vc[0:sl, lane : 2 * lane] = i_
    vc[sl : 2 * sl, 0:lane] = -i_
    vc[sl : 2 * sl, lane : 2 * lane] = r_
    n_rows = GROUP * blocks
    out_row = iota((n_rows, n_rows), 0)
    in_row = iota((n_rows, n_rows), 1)
    spot = in_row // nc % GROUP * blocks + in_row % nc * nab + in_row // (nc * GROUP)
    permt[...] = (spot == out_row).astype(F32).astype(BF)
    settle(kg.at[pl.ds(0, nc - 1)], 5)
    kall = kg[...].reshape(nc * 16, 2 * lane)
    krow = iota((chunks * GROUP * nc, nc * 16), 0)
    kcol = iota((chunks * GROUP * nc, nc * 16), 1)
    pick = (krow % nc * 16 + krow // nc == kcol).astype(F32).astype(BF)
    kd[...] = nn(pick, kall).reshape(chunks, GROUP * nc, 2 * lane)
    lo8 = iota((pair_rows, lane), 1) < frames
    top = iota((pair_rows, lane), 0) < nc

    def hybrids(k, pair):
        at = pair * 2 * sl
        return jnp.concatenate(
            [hr[k, :, p, :, at : at + 2 * sl].reshape(width, 2 * sl) for p in range(2)], 1
        )

    def residual(k):
        settle(zr.at[k, pl.ds(0, nc - 1)], 7 + k)
        total = zr[k, 0].astype(F32)
        for j in range(1, nc):
            total = total + zr[k, j].astype(F32)
        ra[k, ab] = (total - kd[k]).astype(BF)

    def gather(k):
        for j in others:
            remote(
                ra.at[k, ab], ra.at[k, ab], send.at[10 + k], recv.at[10 + k], peer_ab(j)
            ).start()

    def factor_part(k):
        whole = ra[k, ab].astype(F32)
        for c4 in range(GROUP):
            at = c4 // 2 * pair_rows
            here = []
            for q in range(2):
                tile = whole[at : at + pair_rows, q * lane : (q + 1) * lane]
                other = pltpu.roll(tile, nc, 0)
                here.append(
                    jnp.where(top, tile, other) if c4 % 2 == 0 else jnp.where(top, other, tile)
                )
            flip = [pltpu.roll(x, frames, 1) for x in here]
            values = []
            for s in range(2):
                for a, b in zip(here, flip):
                    x = jnp.where(lo8, a, b) if s == 0 else jnp.where(lo8, b, a)
                    values.append((jnp.where(upper[s], 0.0, x), jnp.where(upper[s], x, 0.0)))
            for i in range(nab):
                p0, i0, p1, i1 = pf[0, 0, i], pf[0, 1, i], pf[1, 0, i], pf[1, 1, i]
                re, im = [], []
                for h in range(2):
                    x0, y0, x1, y1 = [v[h] for v in values]
                    re.append((p0 * x0 + i0 * y0) + (p1 * x1 + i1 * y1))
                    im.append((p0 * y0 - i0 * x0) + (p1 * y1 - i1 * x1))
                row = c4 * width + i * 2 * pair_rows
                ef[row : row + 2 * pair_rows, 0:lane] = jnp.concatenate(re, 0).astype(BF)
                ef[row : row + 2 * pair_rows, lane : 2 * lane] = jnp.concatenate(im, 0).astype(BF)
        gv[...] += nn(hrt[k], ef[...])

    def turn(k):
        for p in range(2):
            t = jnp.transpose(hr[k, :, p].reshape(width, GROUP * sl))
            for c4 in range(GROUP):
                hrt[k, p * sl : (p + 1) * sl, c4 * width : (c4 + 1) * width] = t[
                    c4 * sl : (c4 + 1) * sl
                ]

    gv[...] = jnp.zeros_like(gv)

    def parts_of(k, carry):
        settle(hr.at[k, pl.ds(0, nab - 1)], 1 + k)
        tiles = []
        for pair in range(GROUP // 2):
            mx[pair] = nt(hybrids(k, pair), vbt[...])
        for pair in range(GROUP // 2):
            got = [[[0.0, 0.0], [0.0, 0.0]], [[0.0, 0.0], [0.0, 0.0]]]
            for i in range(nab):
                row = i * 2 * pair_rows
                phase = [[pf[s, q, i] for q in range(2)] for s in range(2)]
                for c2 in range(2):
                    low, high = [
                        [
                            mx[
                                pair,
                                row + h * pair_rows : row + (h + 1) * pair_rows,
                                (2 * q + c2) * lane : (2 * q + c2 + 1) * lane,
                            ]
                            for q in range(2)
                        ]
                        for h in range(2)
                    ]
                    for s in range(2):
                        mr = jnp.where(upper[s], high[0], low[0])
                        mi = jnp.where(upper[s], high[1], low[1])
                        pr, pi = phase[s]
                        got[c2][s][0] = got[c2][s][0] + (pr * mr - pi * mi)
                        got[c2][s][1] = got[c2][s][1] + (pr * mi + pi * mr)
            totals = []
            for c2 in range(2):
                both_q = []
                for q in range(2):
                    keep = jnp.where(lo8, got[c2][0][q], got[c2][1][q])
                    fold = jnp.where(lo8, got[c2][1][q], got[c2][0][q])
                    total = keep + pltpu.roll(fold, frames, 1)
                    both_q.append(total + pltpu.roll(total, nc, 0))
                totals.append(both_q)
            tiles.append(
                jnp.concatenate([jnp.where(top, totals[0][q], totals[1][q]) for q in range(2)], 1)
            )
        zr[k, ic] = jnp.concatenate(tiles, 0).astype(BF)
        for j in range(1, nc):
            remote(
                zr.at[k, ic], zr.at[k, ic], send.at[7 + k], recv.at[7 + k], peer_c(j)
            ).start()
        turn(k)

        @pl.when(k >= 1)
        def _():
            residual(k - 1)
            factor_part(k - 1)

        return carry

    lax.fori_loop(0, chunks, parts_of, 0)
    for k in range(chunks - 1):
        gather(k)
    settle(lg.at[:, pl.ds(0, nab - 1)], 6)
    lo = iota((blocks, lane), 1) < frames
    both = lg[...].reshape(blocks, lane)
    zpos = me * slab + iota((blocks, lane), 1) // frames
    for s in range(2):
        mine = lax.rem(both, cells) if s == 0 else lax.div(both, cells)
        kz = lax.rem(mine, depth)
        rowid[s] = lax.div(mine, depth)
        angle = lax.rem(kz * zpos, depth).astype(F32) * (2.0 * math.pi / depth)
        ph[s, 0] = (jnp.cos(angle) * norm).astype(BF).astype(F32)
        ph[s, 1] = (jnp.sin(angle) * -norm).astype(BF).astype(F32)
    residual(chunks - 1)
    gather(chunks - 1)
    factor_part(chunks - 1)

    own = {}
    for p in range(2):
        for q in range(2):
            first = gv[p * sl : p * sl + rank, q * lane : (q + 1) * lane]
            second = gv[p * sl + rank : (p + 1) * sl, q * lane : (q + 1) * lane]
            own[p, q] = first + pltpu.roll(second, frames, 1)
    gre = (own[0, 0] + own[1, 1]) * scale
    gim = (own[0, 1] - own[1, 0]) * scale
    turned = jnp.transpose(jnp.concatenate([gre, gim, gre, gim], 0))
    half = span // 2
    first_half = iota((half, 4 * rank), 1) < 2 * rank
    for f in range(nf):
        gs[f] = jnp.where(
            first_half,
            turned[f * span : f * span + half],
            turned[f * span + half : (f + 1) * span],
        ).astype(BF)
    spot_cf = ic * nf + fr
    gz[spot_cf] = gs[fr]
    for j in range(1, nc * nf):
        remote(
            gs.at[lax.rem(fr + j % nf, nf)], gz.at[spot_cf], send.at[13], recv.at[13], peer_cf(j)
        ).start()
    def spread(k, carry):
        @pl.when(k == chunks - 1)
        def _():
            settle(gz.at[pl.ds(0, nc * nf - 1)], 13)
            gx[ab] = jnp.sum(gz[...].astype(F32), 0)
            for j in others:
                remote(gx.at[ab], gx.at[ab], send.at[14], recv.at[14], peer_ab(j)).start()

        settle(ra.at[k, pl.ds(0, nab - 1)], 10 + k)
        resid = nn(permt[...], ra[k].reshape(n_rows, 2 * lane))
        for c4 in range(GROUP):
            here = [
                resid[c4 * blocks : (c4 + 1) * blocks, q * lane : (q + 1) * lane] for q in range(2)
            ]
            flip = [pltpu.roll(x, frames, 1) for x in here]
            terms = []
            for s in range(2):
                xr_, xi_ = [
                    jnp.where(lo, a, b) if s == 0 else jnp.where(lo, b, a)
                    for a, b in zip(here, flip)
                ]
                pr, pi = ph[s, 0], ph[s, 1]
                terms.append((xr_ * pr + xi_ * pi, xi_ * pr - xr_ * pi))
            for r in range(ROWS):
                m0, m1 = rowid[0] == r, rowid[1] == r
                for q in range(2):
                    ea[k, c4, r * blocks : (r + 1) * blocks, q * lane : (q + 1) * lane] = (
                        jnp.where(m0, terms[0][q], 0.0) + jnp.where(m1, terms[1][q], 0.0)
                    ).astype(BF)
        return carry

    lax.fori_loop(0, chunks, spread, 0)

    def backward(k, carry):
        for c4 in range(GROUP):
            zc = nt(vc[...], ea[k, c4]).astype(BF)
            zg[k, c4 * sl : (c4 + 1) * sl, 0:width] = zc[0:sl]
            zg[k, c4 * sl : (c4 + 1) * sl, width : 2 * width] = zc[sl : 2 * sl]
        back = nn(zg[k], t2_ref[...])
        out = list(carry)
        for z in range(slab):
            re, im = out[2 * z], out[2 * z + 1]
            for c4 in range(GROUP):
                c = k * GROUP + c4
                mr, mi = mf[c, z : z + 1, :], mf[coils + c, z : z + 1, :]
                at = (c4 * slab + z) * rank
                br = back[at : at + rank, 0:width]
                bi = back[at : at + rank, width : 2 * width]
                re = re + mr * br + mi * bi
                im = im + mr * bi - mi * br
            out[2 * z], out[2 * z + 1] = re, im
        return tuple(out)

    zero = jnp.zeros((rank, width), F32)
    out = lax.fori_loop(0, chunks, backward, (zero,) * (2 * slab))
    for z in range(slab):
        for p in range(2):
            gout[p * rank : (p + 1) * rank, z] = out[2 * z + p].reshape(rank, 1, width)
    settle(gx.at[pl.ds(0, nab - 1)], 14)
    total = jnp.sum(gx[...], 0)
    for q in range(2):
        for h in range(2):
            at = (2 * h + q) * rank
            fo[q, h * half : (h + 1) * half, :] = total[:, at : at + rank]


def finish(g_in, f_in, g_out, f_out, sems):
    copies = [
        pltpu.make_async_copy(g_in, g_out, sems.at[0]),
        pltpu.make_async_copy(f_in, f_out, sems.at[1]),
    ]
    for copy in copies:
        copy.start()
    for copy in copies:
        copy.wait()


SHAPES = {64: (4, 4, 4), 8: (2, 2, 2)}


def body(basis, coil_maps, factors, lines, kdata):
    n_cuts = lax.axis_size("cuts")
    nf = lax.axis_size("frame")
    na, nb, nc = SHAPES[n_cuts]
    rank, slab, width = basis.shape[1], basis.shape[2], basis.shape[4]
    coils = coil_maps.shape[1]
    chunks = coils // GROUP
    span = factors.shape[2]
    lpd = lines.shape[1]
    frames = span * nf
    lane = 2 * frames
    sl = slab * rank
    blocks = n_cuts
    n_rows = GROUP * blocks
    scale = 1.0 / math.sqrt(coils * lpd * n_cuts * basis.shape[3] * nf)
    table, table2 = (jnp.asarray(x, BF) for x in real_table(width, (na, nb, nc)))
    b = basis.transpose(0, 1, 3, 2, 4).reshape(2 * rank, slab, width)
    m = coil_maps.transpose(0, 1, 3, 2, 4).reshape(2 * coils, slab, width)
    v = factors.transpose(0, 2, 1)
    l = lines.T
    d = kdata.transpose(0, 3, 4, 2, 1).reshape(2 * coils, lpd, frames)
    dma = pltpu.SemaphoreType.DMA
    vm = pltpu.VMEM
    nab = na * nb
    scratch = [
        vm(b.shape, BF),
        vm(m.shape, BF),
        vm(l.shape, I32),
        vm(d.shape, BF),
        vm(table.shape, BF),
        vm(table.shape, BF),
        vm((slab, 2, rank, width), F32),
        vm(m.shape, F32),
        vm((1, lane), I32),
        vm((2 * nc, 1, lane), I32),
        vm((16, 2 * lane), F32),
        vm((chunks, GROUP * sl, 2 * width), BF),
        vm((chunks, nab, 2, ROWS * nc, GROUP * sl), BF),
        vm((chunks, nab, 2, ROWS * nc, GROUP * sl), BF),
        vm((8 * frames, 8 * rank), BF),
        vm((2 * sl, 2 * lane), BF),
        vm((2, 2, nab, 2 * nc, lane), F32),
        vm((2, 2, blocks, lane), F32),
        vm((2, blocks, lane), I32),
        vm((n_rows, n_rows), BF),
        vm((chunks, nc, GROUP * nc, 2 * lane), BF),
        vm((chunks, nab, GROUP * nc, 2 * lane), BF),
        vm((nc, nab, 1, lane), I32),
        vm((nf, 2, span, rank), BF),
        vm((nc, 16, 2 * lane), BF),
        vm((chunks, GROUP * nc, 2 * lane), F32),
        vm((chunks, GROUP, width, 2 * lane), BF),
        vm((chunks, GROUP * sl, 2 * width), BF),
        vm((2 * sl, 2 * lane), F32),
        vm((chunks, 2 * sl, GROUP * width), BF),
        vm((GROUP * width, 2 * lane), BF),
        vm((2, width, 4 * lane), F32),
        vm((nf, span // 2, 4 * rank), BF),
        vm((nc * nf, span // 2, 4 * rank), BF),
        vm((nab, span // 2, 4 * rank), F32),
        dma((7,)),
        dma((15,)),
        dma((15,)),
    ]
    grad, fg = pl.pallas_call(
        functools.partial(kernel, (na, nb, nc, nf, chunks), scale),
        out_shape=(
            pltpu.VMEM((2 * rank, slab, 1, width), F32),
            pltpu.VMEM((2, span, rank), F32),
        ),
        in_specs=[pl.BlockSpec(memory_space=pl.ANY)] * 7,
        out_specs=[pl.BlockSpec(memory_space=pltpu.VMEM)] * 2,
        scratch_shapes=scratch,
        compiler_params=pltpu.CompilerParams(
            collective_id=0, has_side_effects=True, vmem_limit_bytes=24 * 1024 * 1024
        ),
    )(*[pltpu.with_memory_space_constraint(x, pltpu.HBM) for x in (b, m, v, l, d, table, table2)])
    grad, fg = pl.pallas_call(
        finish,
        out_shape=(
            jax.ShapeDtypeStruct(grad.shape, F32),
            jax.ShapeDtypeStruct(fg.shape, F32),
        ),
        in_specs=[pl.BlockSpec(memory_space=pl.ANY)] * 2,
        out_specs=[pl.BlockSpec(memory_space=pl.ANY)] * 2,
        scratch_shapes=[dma((2,))],
        compiler_params=pltpu.CompilerParams(vmem_limit_bytes=4 * 1024 * 1024),
    )(grad, fg)
    return grad.reshape(basis.shape), fg.transpose(0, 2, 1)


def solution(mesh):
    placed = (
        P(None, None, "cuts", "frame", None),
        P(None, None, "cuts", "frame", None),
        P(None, None, "frame"),
        P(None, "cuts"),
        P(None, None, "cuts", None, "frame"),
    )
    return jax.shard_map(
        body,
        mesh=mesh,
        in_specs=placed,
        out_specs=(P(None, None, "cuts", "frame", None), P(None, None, "frame")),
        check_vma=False,
    )
```

```python
import functools
import math

import jax
import jax.numpy as jnp
import numpy as np
from jax import lax
from jax.experimental import pallas as pl
from jax.experimental.pallas import tpu as pltpu
from jax.sharding import PartitionSpec as P

BF = jnp.bfloat16
F32 = jnp.float32
I32 = jnp.int32
GROUP = 4
ROWS = 4


def real_table(size, shape):
    index = np.arange(size)
    angle = (index[:, None] * index[None, :] % size) * (2.0 * math.pi / size)
    cosine, sine = np.cos(angle) / math.sqrt(size), np.sin(angle) / math.sqrt(size)
    whole = np.stack([np.concatenate([cosine, sine], 1), np.concatenate([-sine, cosine], 1)])
    whole = whole.reshape((2,) + tuple(shape) + (ROWS, 2 * size))
    first = whole.transpose(1, 2, 0, 4, 3, 5).reshape(2 * size, 2 * size)
    second = whole.transpose(0, 4, 3, 1, 2, 5).reshape(2 * size, 2 * size)
    return first, second


def nn(a, b):
    return jnp.dot(a, b, preferred_element_type=F32)


def nt(a, b):
    return lax.dot_general(a, b, (((1,), (1,)), ((), ())), preferred_element_type=F32)


def iota(shape, axis):
    return lax.broadcasted_iota(I32, shape, axis)


def kernel(
    dims,
    scale,
    b_hbm,
    m_hbm,
    v_hbm,
    l_hbm,
    d_hbm,
    t_hbm,
    t2_hbm,
    gout,
    fo,
    bv,
    mv,
    lv,
    dv,
    t_ref,
    t2_ref,
    bf,
    mf,
    lt,
    l8,
    kt,
    img,
    ht,
    hr,
    vbt,
    vc,
    pf,
    ph,
    rowid,
    permt,
    zr,
    ra,
    lg,
    vg,
    kg,
    kd,
    ea,
    zg,
    gv,
    hrt,
    ef,
    mx,
    gs,
    gz,
    gx,
    local,
    send,
    recv,
):
    na, nb, nc, nf, chunks = dims
    coils = chunks * GROUP
    rank = b_hbm.shape[0] // 2
    slab, width = b_hbm.shape[1:]
    span = v_hbm.shape[1]
    frames = span * nf
    nab = na * nb
    blocks = nab * nc
    depth = slab * blocks
    cells = depth * ROWS
    me = lax.axis_index("cuts")
    fr = lax.axis_index("frame")
    ia, ib, ic = me // (nb * nc), (me // nc) % nb, me % nc
    ab = ia * nb + ib
    lane = 2 * frames
    sl = slab * rank
    mesh_id = pl.DeviceIdType.MESH

    def cut(a, b, c):
        return a * (nb * nc) + b * nc + c

    def peer_c(j):
        return {"cuts": cut(ia, ib, lax.rem(ic + j, nc))}

    def peer_f(j):
        return {"frame": lax.rem(fr + j, nf)}

    def peer_ab(j):
        return {"cuts": cut(lax.rem(ia + j // nb, na), lax.rem(ib + j % nb, nb), ic)}

    def peer_cf(j):
        return {
            "cuts": cut(ia, ib, lax.rem(ic + j // nf, nc)),
            "frame": lax.rem(fr + j % nf, nf),
        }

    def remote(src, dst, s, r, who):
        return pltpu.make_async_remote_copy(
            src_ref=src, dst_ref=dst, send_sem=s, recv_sem=r, device_id=who, device_id_type=mesh_id
        )

    def far(j):
        da, db = j // nb, j % nb
        da, db = min(da, na - da), min(db, nb - db)
        return (-da, -db, j)

    others = sorted(range(1, nab), key=far)
    everyone = [peer_ab(j) for j in others] + [peer_cf(j) for j in range(1, nc * nf)]
    barrier = pltpu.get_barrier_semaphore()
    for who in everyone:
        pl.semaphore_signal(barrier, inc=1, device_id=who, device_id_type=mesh_id)

    def settle(block, at):
        pltpu.make_async_copy(block, block, send.at[at]).wait()
        pltpu.make_async_copy(block, block, recv.at[at]).wait()

    loads = [
        pltpu.make_async_copy(l_hbm, lv, local.at[0]),
        pltpu.make_async_copy(b_hbm, bv, local.at[1]),
        pltpu.make_async_copy(m_hbm, mv, local.at[2]),
        pltpu.make_async_copy(t_hbm, t_ref, local.at[3]),
        pltpu.make_async_copy(v_hbm, vg.at[fr], local.at[4]),
        pltpu.make_async_copy(d_hbm, dv, local.at[5]),
        pltpu.make_async_copy(t2_hbm, t2_ref, local.at[6]),
    ]
    for copy in loads:
        copy.start()
    loads[0].wait()
    row = lv[0:1, :] + lv[1:2, :] * cells
    lt[0:1, 0:frames] = row
    lt[0:1, frames:lane] = row
    lg[ic, pl.ds(ab, 1)] = lt[...][None]
    loads[1].wait()
    loads[2].wait()
    for p in range(2):
        x = bv[p * rank : (p + 1) * rank].astype(F32)
        for z in range(slab):
            bf[z, p] = x[:, z, :]
    mf[...] = mv[...].astype(F32)
    loads[3].wait()
    loads[4].wait()

    def forward(k, carry):
        for c4 in range(GROUP):
            c = k * GROUP + c4
            for z in range(slab):
                mr, mi = mf[c, z : z + 1, :], mf[coils + c, z : z + 1, :]
                br, bi = bf[z, 0], bf[z, 1]
                at = (c4 * slab + z) * rank
                img[k, at : at + rank, 0:width] = (mr * br - mi * bi).astype(BF)
                img[k, at : at + rank, width : 2 * width] = (mr * bi + mi * br).astype(BF)
        ht[k] = nt(t_ref[...], img[k]).astype(BF).reshape(nab, 2, ROWS * nc, GROUP * sl)
        hr[k, ab] = ht[k, ab]
        return carry

    lax.fori_loop(0, chunks, forward, 0)

    pl.semaphore_wait(barrier, len(everyone))

    for j in range(1, nc):
        own_line = lg.at[ic, pl.ds(ab, 1)]
        remote(own_line, own_line, send.at[0], recv.at[0], peer_c(j)).start()
    def exchange(k):
        for j in sorted(others, key=lambda j: (far(j)[0] + far(j)[1], j * 7 % nab)):
            to = lax.rem(ia + j // nb, na) * nb + lax.rem(ib + j % nb, nb)
            remote(
                ht.at[k, to], hr.at[k, ab], send.at[1 + k], recv.at[1 + k], peer_ab(j)
            ).start()

    exchange(0)

    @pl.when(lax.rem(fr, 2) == 0)
    def _():
        for k in range(1, chunks):
            exchange(k)

    for j in range(1, nf):
        remote(vg.at[fr], vg.at[fr], send.at[4], recv.at[4], peer_f(j)).start()
    loads[5].wait()
    kt[...] = jnp.zeros_like(kt)
    for q in range(2):
        x = dv[q * coils : (q + 1) * coils].astype(F32)
        for s in range(2):
            kt[0:coils, q * lane + s * frames : q * lane + (s + 1) * frames] = x[:, s, :]
    kg[ic] = kt[...].astype(BF)
    for j in range(1, nc):
        remote(kg.at[ic], kg.at[ic], send.at[5], recv.at[5], peer_c(j)).start()
    loads[6].wait()
    settle(lg.at[pl.ds(0, nc - 1), pl.ds(0, 1)], 0)
    for j in others:
        mine = lg.at[:, pl.ds(ab, 1)]
        remote(mine, mine, send.at[6], recv.at[6], peer_ab(j)).start()

    @pl.when(lax.rem(fr, 2) == 1)
    def _():
        for k in range(1, chunks):
            exchange(k)

    pair_rows = 2 * nc
    l8[0:nc] = lg[:, ab]
    l8[nc:pair_rows] = lg[:, ab]
    both = l8[...].reshape(pair_rows, lane)
    norm = 1.0 / math.sqrt(depth)
    odd = iota((pair_rows, lane), 0) // nc
    zlane = iota((pair_rows, lane), 1) // frames
    upper = []
    for s in range(2):
        mine = lax.rem(both, cells) if s == 0 else lax.div(both, cells)
        kz = lax.rem(mine, depth)
        r = lax.div(mine, depth)
        upper.append(r >= 2)
        here = lax.rem(r, 2) == odd
        for i in range(nab):
            zpos = (i * nc + ic) * slab + zlane
            angle = lax.rem(kz * zpos, depth).astype(F32) * (2.0 * math.pi / depth)
            pf[s, 0, i] = jnp.where(here, (jnp.cos(angle) * norm).astype(BF).astype(F32), 0.0)
            pf[s, 1, i] = jnp.where(here, (jnp.sin(angle) * -norm).astype(BF).astype(F32), 0.0)
    settle(vg.at[pl.ds(0, nf - 1)], 4)

    vt = [vg[:, p].reshape(frames, rank) for p in range(2)]
    rep = (iota((rank, 4 * rank), 0) == iota((rank, 4 * rank), 1) % rank).astype(F32).astype(BF)
    wide = [nn(vt[p], rep) for p in range(2)]
    block_of = iota((frames, 4 * rank), 1) // rank
    for blk in range(4):
        r_ = jnp.where(block_of == blk, wide[0], 0.0).astype(BF)
        i_ = jnp.where(block_of == blk, wide[1], 0.0).astype(BF)
        at = blk * frames
        vbt[at : at + frames, 0 : 4 * rank] = r_
        vbt[at : at + frames, 4 * rank : 8 * rank] = -i_
        at = (4 + blk) * frames
        vbt[at : at + frames, 0 : 4 * rank] = i_
        vbt[at : at + frames, 4 * rank : 8 * rank] = r_
    rep2 = (iota((sl, rank), 0) % rank == iota((sl, rank), 1)).astype(F32).astype(BF)
    same = iota((sl, lane), 0) // rank == iota((sl, lane), 1) // frames
    tall = [nt(rep2, jnp.concatenate([vt[p], vt[p]], 0)) for p in range(2)]
    r_ = jnp.where(same, tall[0], 0.0).astype(BF)
    i_ = jnp.where(same, tall[1], 0.0).astype(BF)
    vc[0:sl, 0:lane] = r_
    vc[0:sl, lane : 2 * lane] = i_
    vc[sl : 2 * sl, 0:lane] = -i_
    vc[sl : 2 * sl, lane : 2 * lane] = r_
    n_rows = GROUP * blocks
    out_row = iota((n_rows, n_rows), 0)
    in_row = iota((n_rows, n_rows), 1)
    spot = in_row // nc % GROUP * blocks + in_row % nc * nab + in_row // (nc * GROUP)
    permt[...] = (spot == out_row).astype(F32).astype(BF)
    settle(kg.at[pl.ds(0, nc - 1)], 5)
    kall = kg[...].reshape(nc * 16, 2 * lane)
    krow = iota((chunks * GROUP * nc, nc * 16), 0)
    kcol = iota((chunks * GROUP * nc, nc * 16), 1)
    pick = (krow % nc * 16 + krow // nc == kcol).astype(F32).astype(BF)
    kd[...] = nn(pick, kall).reshape(chunks, GROUP * nc, 2 * lane)
    lo8 = iota((pair_rows, lane), 1) < frames
    top = iota((pair_rows, lane), 0) < nc

    def hybrids(k, pair):
        at = pair * 2 * sl
        return jnp.concatenate(
            [hr[k, :, p, :, at : at + 2 * sl].reshape(width, 2 * sl) for p in range(2)], 1
        )

    def residual(k):
        settle(zr.at[k, pl.ds(0, nc - 1)], 7 + k)
        total = zr[k, 0].astype(F32)
        for j in range(1, nc):
            total = total + zr[k, j].astype(F32)
        ra[k, ab] = (total - kd[k]).astype(BF)

    def gather(k):
        for j in others:
            remote(
                ra.at[k, ab], ra.at[k, ab], send.at[10 + k], recv.at[10 + k], peer_ab(j)
            ).start()

    def factor_part(k):
        whole = ra[k, ab].astype(F32)
        for c4 in range(GROUP):
            at = c4 // 2 * pair_rows
            here = []
            for q in range(2):
                tile = whole[at : at + pair_rows, q * lane : (q + 1) * lane]
                other = pltpu.roll(tile, nc, 0)
                here.append(
                    jnp.where(top, tile, other) if c4 % 2 == 0 else jnp.where(top, other, tile)
                )
            flip = [pltpu.roll(x, frames, 1) for x in here]
            values = []
            for s in range(2):
                for a, b in zip(here, flip):
                    x = jnp.where(lo8, a, b) if s == 0 else jnp.where(lo8, b, a)
                    values.append((jnp.where(upper[s], 0.0, x), jnp.where(upper[s], x, 0.0)))
            for i in range(nab):
                p0, i0, p1, i1 = pf[0, 0, i], pf[0, 1, i], pf[1, 0, i], pf[1, 1, i]
                re, im = [], []
                for h in range(2):
                    x0, y0, x1, y1 = [v[h] for v in values]
                    re.append((p0 * x0 + i0 * y0) + (p1 * x1 + i1 * y1))
                    im.append((p0 * y0 - i0 * x0) + (p1 * y1 - i1 * x1))
                row = c4 * width + i * 2 * pair_rows
                ef[row : row + 2 * pair_rows, 0:lane] = jnp.concatenate(re, 0).astype(BF)
                ef[row : row + 2 * pair_rows, lane : 2 * lane] = jnp.concatenate(im, 0).astype(BF)
        gv[...] += nn(hrt[k], ef[...])

    def turn(k):
        for p in range(2):
            t = jnp.transpose(hr[k, :, p].reshape(width, GROUP * sl))
            for c4 in range(GROUP):
                hrt[k, p * sl : (p + 1) * sl, c4 * width : (c4 + 1) * width] = t[
                    c4 * sl : (c4 + 1) * sl
                ]

    gv[...] = jnp.zeros_like(gv)

    def parts_of(k, carry):
        settle(hr.at[k, pl.ds(0, nab - 1)], 1 + k)
        tiles = []
        for pair in range(GROUP // 2):
            mx[pair] = nt(hybrids(k, pair), vbt[...])
        for pair in range(GROUP // 2):
            got = [[[0.0, 0.0], [0.0, 0.0]], [[0.0, 0.0], [0.0, 0.0]]]
            for i in range(nab):
                row = i * 2 * pair_rows
                phase = [[pf[s, q, i] for q in range(2)] for s in range(2)]
                for c2 in range(2):
                    low, high = [
                        [
                            mx[
                                pair,
                                row + h * pair_rows : row + (h + 1) * pair_rows,
                                (2 * q + c2) * lane : (2 * q + c2 + 1) * lane,
                            ]
                            for q in range(2)
                        ]
                        for h in range(2)
                    ]
                    for s in range(2):
                        mr = jnp.where(upper[s], high[0], low[0])
                        mi = jnp.where(upper[s], high[1], low[1])
                        pr, pi = phase[s]
                        got[c2][s][0] = got[c2][s][0] + (pr * mr - pi * mi)
                        got[c2][s][1] = got[c2][s][1] + (pr * mi + pi * mr)
            totals = []
            for c2 in range(2):
                both_q = []
                for q in range(2):
                    keep = jnp.where(lo8, got[c2][0][q], got[c2][1][q])
                    fold = jnp.where(lo8, got[c2][1][q], got[c2][0][q])
                    total = keep + pltpu.roll(fold, frames, 1)
                    both_q.append(total + pltpu.roll(total, nc, 0))
                totals.append(both_q)
            tiles.append(
                jnp.concatenate([jnp.where(top, totals[0][q], totals[1][q]) for q in range(2)], 1)
            )
        zr[k, ic] = jnp.concatenate(tiles, 0).astype(BF)
        for j in range(1, nc):
            remote(
                zr.at[k, ic], zr.at[k, ic], send.at[7 + k], recv.at[7 + k], peer_c(j)
            ).start()
        turn(k)

        @pl.when(k >= 1)
        def _():
            residual(k - 1)
            factor_part(k - 1)

        return carry

    lax.fori_loop(0, chunks, parts_of, 0)
    for k in range(chunks - 1):
        gather(k)
    settle(lg.at[:, pl.ds(0, nab - 1)], 6)
    lo = iota((blocks, lane), 1) < frames
    both = lg[...].reshape(blocks, lane)
    zpos = me * slab + iota((blocks, lane), 1) // frames
    for s in range(2):
        mine = lax.rem(both, cells) if s == 0 else lax.div(both, cells)
        kz = lax.rem(mine, depth)
        rowid[s] = lax.div(mine, depth)
        angle = lax.rem(kz * zpos, depth).astype(F32) * (2.0 * math.pi / depth)
        ph[s, 0] = (jnp.cos(angle) * norm).astype(BF).astype(F32)
        ph[s, 1] = (jnp.sin(angle) * -norm).astype(BF).astype(F32)
    residual(chunks - 1)
    gather(chunks - 1)
    factor_part(chunks - 1)

    own = {}
    for p in range(2):
        for q in range(2):
            first = gv[p * sl : p * sl + rank, q * lane : (q + 1) * lane]
            second = gv[p * sl + rank : (p + 1) * sl, q * lane : (q + 1) * lane]
            own[p, q] = first + pltpu.roll(second, frames, 1)
    gre = (own[0, 0] + own[1, 1]) * scale
    gim = (own[0, 1] - own[1, 0]) * scale
    turned = jnp.transpose(jnp.concatenate([gre, gim, gre, gim], 0))
    half = span // 2
    first_half = iota((half, 4 * rank), 1) < 2 * rank
    for f in range(nf):
        gs[f] = jnp.where(
            first_half,
            turned[f * span : f * span + half],
            turned[f * span + half : (f + 1) * span],
        ).astype(BF)
    spot_cf = ic * nf + fr
    gz[spot_cf] = gs[fr]
    for j in range(1, nc * nf):
        remote(
            gs.at[lax.rem(fr + j % nf, nf)], gz.at[spot_cf], send.at[13], recv.at[13], peer_cf(j)
        ).start()
    def spread(k, carry):
        @pl.when(k == chunks - 1)
        def _():
            settle(gz.at[pl.ds(0, nc * nf - 1)], 13)
            gx[ab] = jnp.sum(gz[...].astype(F32), 0)
            for j in others:
                remote(gx.at[ab], gx.at[ab], send.at[14], recv.at[14], peer_ab(j)).start()

        settle(ra.at[k, pl.ds(0, nab - 1)], 10 + k)
        resid = nn(permt[...], ra[k].reshape(n_rows, 2 * lane))
        for c4 in range(GROUP):
            here = [
                resid[c4 * blocks : (c4 + 1) * blocks, q * lane : (q + 1) * lane] for q in range(2)
            ]
            flip = [pltpu.roll(x, frames, 1) for x in here]
            terms = []
            for s in range(2):
                xr_, xi_ = [
                    jnp.where(lo, a, b) if s == 0 else jnp.where(lo, b, a)
                    for a, b in zip(here, flip)
                ]
                pr, pi = ph[s, 0], ph[s, 1]
                terms.append((xr_ * pr + xi_ * pi, xi_ * pr - xr_ * pi))
            for r in range(ROWS):
                m0, m1 = rowid[0] == r, rowid[1] == r
                for q in range(2):
                    ea[k, c4, r * blocks : (r + 1) * blocks, q * lane : (q + 1) * lane] = (
                        jnp.where(m0, terms[0][q], 0.0) + jnp.where(m1, terms[1][q], 0.0)
                    ).astype(BF)
        return carry

    lax.fori_loop(0, chunks, spread, 0)

    def backward(k, carry):
        for c4 in range(GROUP):
            zc = nt(vc[...], ea[k, c4]).astype(BF)
            zg[k, c4 * sl : (c4 + 1) * sl, 0:width] = zc[0:sl]
            zg[k, c4 * sl : (c4 + 1) * sl, width : 2 * width] = zc[sl : 2 * sl]
        back = nn(zg[k], t2_ref[...])
        out = list(carry)
        for z in range(slab):
            re, im = out[2 * z], out[2 * z + 1]
            for c4 in range(GROUP):
                c = k * GROUP + c4
                mr, mi = mf[c, z : z + 1, :], mf[coils + c, z : z + 1, :]
                at = (c4 * slab + z) * rank
                br = back[at : at + rank, 0:width]
                bi = back[at : at + rank, width : 2 * width]
                re = re + mr * br + mi * bi
                im = im + mr * bi - mi * br
            out[2 * z], out[2 * z + 1] = re, im
        return tuple(out)

    zero = jnp.zeros((rank, width), F32)
    out = lax.fori_loop(0, chunks, backward, (zero,) * (2 * slab))
    for z in range(slab):
        for p in range(2):
            gout[p * rank : (p + 1) * rank, z] = out[2 * z + p].reshape(rank, 1, width)
    settle(gx.at[pl.ds(0, nab - 1)], 14)
    total = jnp.sum(gx[...], 0)
    for q in range(2):
        for h in range(2):
            at = (2 * h + q) * rank
            fo[q, h * half : (h + 1) * half, :] = total[:, at : at + rank]


def finish(g_in, f_in, g_out, f_out, sems):
    copies = [
        pltpu.make_async_copy(g_in, g_out, sems.at[0]),
        pltpu.make_async_copy(f_in, f_out, sems.at[1]),
    ]
    for copy in copies:
        copy.start()
    for copy in copies:
        copy.wait()


SHAPES = {64: (4, 4, 4), 8: (2, 2, 2)}


def body(basis, coil_maps, factors, lines, kdata):
    n_cuts = lax.axis_size("cuts")
    nf = lax.axis_size("frame")
    na, nb, nc = SHAPES[n_cuts]
    rank, slab, width = basis.shape[1], basis.shape[2], basis.shape[4]
    coils = coil_maps.shape[1]
    chunks = coils // GROUP
    span = factors.shape[2]
    lpd = lines.shape[1]
    frames = span * nf
    lane = 2 * frames
    sl = slab * rank
    blocks = n_cuts
    n_rows = GROUP * blocks
    scale = 1.0 / math.sqrt(coils * lpd * n_cuts * basis.shape[3] * nf)
    table, table2 = (jnp.asarray(x, BF) for x in real_table(width, (na, nb, nc)))
    b = basis.transpose(0, 1, 3, 2, 4).reshape(2 * rank, slab, width)
    m = coil_maps.transpose(0, 1, 3, 2, 4).reshape(2 * coils, slab, width)
    v = factors.transpose(0, 2, 1)
    l = lines.T
    d = kdata.transpose(0, 3, 4, 2, 1).reshape(2 * coils, lpd, frames)
    dma = pltpu.SemaphoreType.DMA
    vm = pltpu.VMEM
    nab = na * nb
    scratch = [
        vm(b.shape, BF),
        vm(m.shape, BF),
        vm(l.shape, I32),
        vm(d.shape, BF),
        vm(table.shape, BF),
        vm(table.shape, BF),
        vm((slab, 2, rank, width), F32),
        vm(m.shape, F32),
        vm((1, lane), I32),
        vm((2 * nc, 1, lane), I32),
        vm((16, 2 * lane), F32),
        vm((chunks, GROUP * sl, 2 * width), BF),
        vm((chunks, nab, 2, ROWS * nc, GROUP * sl), BF),
        vm((chunks, nab, 2, ROWS * nc, GROUP * sl), BF),
        vm((8 * frames, 8 * rank), BF),
        vm((2 * sl, 2 * lane), BF),
        vm((2, 2, nab, 2 * nc, lane), F32),
        vm((2, 2, blocks, lane), F32),
        vm((2, blocks, lane), I32),
        vm((n_rows, n_rows), BF),
        vm((chunks, nc, GROUP * nc, 2 * lane), BF),
        vm((chunks, nab, GROUP * nc, 2 * lane), BF),
        vm((nc, nab, 1, lane), I32),
        vm((nf, 2, span, rank), BF),
        vm((nc, 16, 2 * lane), BF),
        vm((chunks, GROUP * nc, 2 * lane), F32),
        vm((chunks, GROUP, width, 2 * lane), BF),
        vm((chunks, GROUP * sl, 2 * width), BF),
        vm((2 * sl, 2 * lane), F32),
        vm((chunks, 2 * sl, GROUP * width), BF),
        vm((GROUP * width, 2 * lane), BF),
        vm((2, width, 4 * lane), F32),
        vm((nf, span // 2, 4 * rank), BF),
        vm((nc * nf, span // 2, 4 * rank), BF),
        vm((nab, span // 2, 4 * rank), F32),
        dma((7,)),
        dma((15,)),
        dma((15,)),
    ]
    grad, fg = pl.pallas_call(
        functools.partial(kernel, (na, nb, nc, nf, chunks), scale),
        out_shape=(
            pltpu.VMEM((2 * rank, slab, 1, width), F32),
            pltpu.VMEM((2, span, rank), F32),
        ),
        in_specs=[pl.BlockSpec(memory_space=pl.ANY)] * 7,
        out_specs=[pl.BlockSpec(memory_space=pltpu.VMEM)] * 2,
        scratch_shapes=scratch,
        compiler_params=pltpu.CompilerParams(
            collective_id=0, has_side_effects=True, vmem_limit_bytes=24 * 1024 * 1024
        ),
    )(*[pltpu.with_memory_space_constraint(x, pltpu.HBM) for x in (b, m, v, l, d, table, table2)])
    grad, fg = pl.pallas_call(
        finish,
        out_shape=(
            jax.ShapeDtypeStruct(grad.shape, F32),
            jax.ShapeDtypeStruct(fg.shape, F32),
        ),
        in_specs=[pl.BlockSpec(memory_space=pl.ANY)] * 2,
        out_specs=[pl.BlockSpec(memory_space=pl.ANY)] * 2,
        scratch_shapes=[dma((2,))],
        compiler_params=pltpu.CompilerParams(vmem_limit_bytes=4 * 1024 * 1024),
    )(grad, fg)
    return grad.reshape(basis.shape), fg.transpose(0, 2, 1)


def solution(mesh):
    placed = (
        P(None, None, "cuts", "frame", None),
        P(None, None, "cuts", "frame", None),
        P(None, None, "frame"),
        P(None, "cuts"),
        P(None, None, "cuts", None, "frame"),
    )
    return jax.shard_map(
        body,
        mesh=mesh,
        in_specs=placed,
        out_specs=(P(None, None, "cuts", "frame", None), P(None, None, "frame")),
        check_vma=False,
    )
```
